32 devices in a mesh: parts: 2 (over y), az: 4 (over z), date: 2 (over x), rg: 2 (over core).
Axes of the slice: x: 2, y: 2, z: 4, core: 2. Of those that a mesh axis runs over, the one named last changes fastest.
Arguments:
- image_stack: float32 [2, 4, 256, 512], P(None, ('parts', 'date'), 'az', 'rg'), parts along dimension 1, may hold values from -6 to 6
- tap_weights: float32 [8, 4, 256], P(None, ('parts', 'date'), 'az'), parts along dimension 1, may hold values from -0.25 to 0.75
- offsets: int32 [4, 256], P(('parts', 'date'), 'az'), parts along dimension 0, may hold values from -12 to 12, as said below
- matchings: int32 [3, 2], replicated, may hold values from 0 to 1, each once within a row
Outputs:
- filtered: float32 [3, 2, 4, 256, 512], P(None, None, ('parts', 'date'), 'az', 'rg'), parts along dimension 2
The draws below stay inside these ranges and needn't reach their ends.
There are 2 independent parts, one for each index of `parts`. The reference program is written for one: setup_inputs(seed, part) draws one part's arguments, and reference() takes and returns one part's arrays. A program takes and returns all parts, laid end to end along the dimension named above; an argument that names none is the same for every part. Nothing has to cross between parts.
Inputs may be any that keep to these rules, and one draw needn't show every extreme that they name: `offsets`: both ends of the range occur in every draw. `matchings`: each row names every date once.
All inputs are finite; a program needn't handle non-finite values.
Results may differ from the reference program's by a relative error of at most 0.0045.
Values may be sent and summed in bfloat16 or wider, within the bound.
A program may use at most 64 MiB of HBM per device.

```python
import math
import jax
import jax.numpy as jnp
from jax import lax

TAPS = 8
SHIFT_MAX = 12
MATCHES = 3
PATCH = 64
DATES = 2
LINES = 256
SAMPLES = 512


def draw_offsets(key, part):
    random_base = jax.random.randint(jax.random.fold_in(key, 11), (DATES * LINES,), -SHIFT_MAX, SHIFT_MAX + 1, dtype=jnp.int32)
    spot_first = jax.random.randint(jax.random.fold_in(key, 12), (), 0, DATES * LINES, dtype=jnp.int32)
    spot_step = jax.random.randint(jax.random.fold_in(key, 13), (), 1, DATES * LINES, dtype=jnp.int32)
    spot_second = (spot_first + spot_step) % (DATES * LINES)
    flat_values = random_base.at[spot_first].set(SHIFT_MAX)
    flat_values = flat_values.at[spot_second].set(-SHIFT_MAX)
    return flat_values.reshape(DATES, LINES)


def steps_of(stream_key, dims, pieces, low, largest):
    factor_of, own = 1.0, jax.random.fold_in(stream_key, 6)
    for axis_at, shards_of in pieces:
        draws = jnp.exp(jax.random.uniform(jax.random.fold_in(own, axis_at), (shards_of,), jnp.float32, low / len(pieces), largest / len(pieces)))
        factor_of = factor_of * jnp.repeat(draws, dims[axis_at] // shards_of).reshape([-1 if axis == axis_at else 1 for axis in range(len(dims))])
    return factor_of


def noise(stream_key, shape, spread, limit, pieces=(), held_as=jnp.bfloat16):
    level = steps_of(stream_key, shape, pieces, -0.22, 0.18) if pieces else 1.0
    values = jax.random.normal(stream_key, shape, jnp.float32) * spread * level
    return jnp.minimum(jnp.maximum(values, -limit), limit).astype(held_as)


def setup_inputs(seed: int = 0, part: int = 0) -> dict:
    streams_of = jax.random.split(jax.random.key(seed), 5)
    own_keys = jax.random.split(jax.random.fold_in(streams_of[4], part), 5)
    return {
        "image_stack": noise(own_keys[0], (2, DATES, LINES, SAMPLES), 1.0, 6.0, ((1, 2), (2, 4), (3, 2)), jnp.float32),
        "tap_weights": jnp.clip(-0.25 + 1.0 * jax.random.uniform(own_keys[1], (TAPS, DATES, LINES), jnp.float32) ** steps_of(own_keys[1], (TAPS, DATES, LINES), ((1, 2), (2, 4)), -0.2, 0.2), -0.25, 0.75),
        "offsets": draw_offsets(jax.random.fold_in(jax.random.fold_in(streams_of[4], part), 71), part),
        "matchings": jax.vmap(lambda own: jax.random.permutation(own, DATES))(jax.random.split(streams_of[3], MATCHES)).reshape((MATCHES, DATES)).astype(jnp.int32),
    }


def fourier_table(sine_sign, table_scale):
    freq_ids = jnp.arange(PATCH, dtype=jnp.int32)
    phase_ids = (freq_ids[:, None] * freq_ids[None, :]) % PATCH
    angles = phase_ids.astype(jnp.float32) * (2.0 * math.pi / PATCH)
    cosine = jnp.cos(angles) * table_scale
    sine_part = jnp.sin(angles) * (sine_sign * table_scale)
    upper_rows = jnp.concatenate([cosine, -sine_part], axis=1)
    bottom = jnp.concatenate([sine_part, cosine], axis=1)
    return jnp.concatenate([upper_rows, bottom], axis=0).astype(jnp.bfloat16)


def patch_window():
    return jnp.sin(math.pi * (jnp.arange(PATCH, dtype=jnp.float32) + 0.5) / PATCH) ** 2


def filter_rows(band_rows, forward_table, inverse_table, window):
    half_patch = PATCH // 2
    width = band_rows.shape[1]
    line_spectra = jnp.dot(forward_table.T, band_rows, preferred_element_type=jnp.float32).astype(jnp.bfloat16)
    blocks = line_spectra.reshape(2, PATCH, width // half_patch, half_patch)
    patches = jnp.concatenate([blocks[:, :, :-1], blocks[:, :, 1:]], axis=3)
    patches = patches.transpose(1, 2, 0, 3).reshape(PATCH, -1, 2 * PATCH)
    spectrum = jnp.dot(patches, forward_table, preferred_element_type=jnp.float32)
    spec_real = spectrum[..., :PATCH]
    spec_imag = spectrum[..., PATCH:]
    power_spec = spec_real * spec_real + spec_imag * spec_imag
    smooth = power_spec + jnp.roll(power_spec, 1, 0) + jnp.roll(power_spec, -1, 0)
    smooth = smooth + jnp.roll(smooth, 1, 2) + jnp.roll(smooth, -1, 2)
    ref_power = PATCH * PATCH * 1.0
    gain_map = jnp.power((smooth / 9.0 + ref_power) / ref_power, 0.25)
    shaped = jnp.concatenate([spec_real * gain_map, spec_imag * gain_map], axis=-1).astype(jnp.bfloat16)
    range_back = jnp.dot(shaped, inverse_table, preferred_element_type=jnp.float32).astype(jnp.bfloat16)
    range_back = range_back.reshape(PATCH, -1, 2, PATCH)
    lines_back = jnp.einsum('lqcs,cldm->mqds', range_back.astype(jnp.float32), inverse_table.reshape(2, PATCH, 2, PATCH).astype(jnp.float32))
    weighted = lines_back * window[:, None, None, None] * window[None, None, None, :]
    joined = weighted[:, :-1, :, half_patch:] + weighted[:, 1:, :, :half_patch]
    return joined.transpose(2, 0, 1, 3).reshape(2, PATCH, -1)


def filter_item(item_slab, forward_table, inverse_table, window):
    half_patch = PATCH // 2
    width = item_slab.shape[2]
    row_count = item_slab.shape[1] // half_patch - 1

    def single_row(row_index):
        band_rows = lax.dynamic_slice_in_dim(item_slab, row_index * half_patch, PATCH, 1).reshape(2 * PATCH, width)
        return filter_rows(band_rows, forward_table, inverse_table, window)

    row_results = lax.map(single_row, jnp.arange(row_count, dtype=jnp.int32))
    joined = row_results[:-1, :, half_patch:] + row_results[1:, :, :half_patch]
    return joined.transpose(1, 0, 2, 3).reshape(2, (row_count - 1) * half_patch, -1)


def reference(image_stack, tap_weights, offsets, matchings):
    rim_width = SHIFT_MAX + TAPS // 2
    padded = jnp.pad(image_stack, ((0, 0), (0, 0), (rim_width, rim_width), (0, 0)))
    line_ids = jnp.arange(LINES, dtype=jnp.int32)
    summed = jnp.zeros(image_stack.shape, jnp.float32)
    for tap_index in range(TAPS):
        source_rows = (line_ids[None, :] + offsets + (tap_index - (TAPS // 2 - 1) + rim_width)).astype(jnp.int32)
        picked = jax.vmap(lambda slab_one, rows_one: jnp.take(slab_one, rows_one, axis=1), in_axes=(1, 0), out_axes=1)(padded, source_rows)
        summed = summed + tap_weights[tap_index][None, :, :, None] * picked
    resampled = summed.astype(jnp.bfloat16)
    own_real = resampled[0].astype(jnp.float32)
    own_imag = resampled[1].astype(jnp.float32)
    products = []
    for match_index in range(MATCHES):
        partner = jnp.take(resampled, matchings[match_index], axis=1)
        other_real = partner[0].astype(jnp.float32)
        other_imag = partner[1].astype(jnp.float32)
        real_part = own_real * other_real + own_imag * other_imag
        imag_part = own_imag * other_real - own_real * other_imag
        products.append(jnp.stack([real_part, imag_part], axis=0))
    interferogram = jnp.stack(products, axis=0).astype(jnp.bfloat16)
    half_patch = PATCH // 2
    padded_ifg = jnp.pad(interferogram, ((0, 0), (0, 0), (0, 0), (half_patch, half_patch), (half_patch, half_patch)))
    items = padded_ifg.transpose(0, 2, 1, 3, 4).reshape(MATCHES * DATES, 2, LINES + PATCH, SAMPLES + PATCH)
    forward_table = fourier_table(1.0, 1.0)
    inverse_table = fourier_table(-1.0, 1.0 / PATCH)
    window = patch_window()
    results = lax.map(lambda item_slab: filter_item(item_slab, forward_table, inverse_table, window), items)
    return results.reshape(MATCHES, DATES, 2, LINES, SAMPLES).transpose(0, 2, 1, 3, 4)
```

```python
import functools
import math

import jax
import jax.numpy as jnp
import ml_dtypes
import numpy as np
from jax import lax
from jax.experimental import pallas as pl
from jax.experimental.pallas import tpu as pltpu
from jax.sharding import PartitionSpec as P

TAPS = 8
SHIFT_MAX = 12
PATCH = 64
HALF = PATCH // 2
RIM = SHIFT_MAX + TAPS // 2
REACH = RIM + HALF
GROUPS = 4
LANES = GROUPS * PATCH
MESH = pl.DeviceIdType.MESH
BF16 = ml_dtypes.bfloat16
PLACE = {1: 0, 0: 1, -1: 2}


def fourier_table(sine_sign, table_scale):
    ids = np.arange(PATCH)
    angles = ((ids[:, None] * ids[None, :]) % PATCH) * (2.0 * math.pi / PATCH)
    cosine = np.cos(angles) * table_scale
    sine = np.sin(angles) * (sine_sign * table_scale)
    table = np.block([[cosine, -sine], [sine, cosine]]).astype(np.float32)
    return table.astype(BF16).astype(np.float32)


def tables():
    forward = fourier_table(1.0, 1.0)
    inverse = fourier_table(-1.0, 1.0 / PATCH)
    window = np.sin(math.pi * (np.arange(PATCH, dtype=np.float32) + 0.5) / PATCH) ** 2
    wide = 2 * PATCH
    line_in = np.zeros((2, wide, 2, GROUPS, PATCH), np.float32)
    line_out = np.zeros((2, PATCH, 2, GROUPS, PATCH), np.float32)
    split_f = forward.reshape(2, PATCH, 2, PATCH)
    split_i = inverse.reshape(2, PATCH, 2, PATCH)
    for r in range(3):
        line_in[:, r * HALF : r * HALF + PATCH, :, r] = split_f
        for line in range(PATCH):
            u = line + HALF - HALF * r
            if 0 <= u < PATCH:
                line_out[:, line, :, r] = split_i[:, :, :, u].transpose(2, 0, 1) * window[u]
    line_in = line_in.reshape(2 * wide, 2 * LANES).astype(BF16)
    line_out = line_out.reshape(wide, 2 * LANES)
    high = line_out.astype(BF16)
    low = (line_out - high.astype(np.float32)).astype(BF16)
    ids = np.arange(LANES)
    gap = (ids[:, None] - ids[None, :]) % PATCH
    same = ids[:, None] // PATCH == ids[None, :] // PATCH
    ring = (((gap <= 1) | (gap == PATCH - 1)) & same).astype(BF16)
    turns = np.concatenate([forward.T, inverse.T], axis=0).astype(BF16)
    rows = np.broadcast_to(np.tile(window, 2)[:, None], (wide, wide)).astype(np.float32)
    rows_high = rows.astype(BF16)
    rows_low = (rows - rows_high.astype(np.float32)).astype(BF16)
    last = np.concatenate([ring, turns, np.concatenate([rows_high, rows_low], axis=0)], axis=1)
    return np.concatenate([line_in, high, low, last], axis=0)


def stack_kernel(
    az_size, date_size, count, image_hbm, taps_hbm, offsets_hbm, table_hbm, *rest,
):
    if count < date_size:
        matchings, *rest = rest
    (
        out, image, taps, offsets, table, tile, pack, kernels, near, far, near_side, far_side,
        all_kernels, turned, spec, power_sum, shaped, back, load_sem, send_sem, recv_sem, ready,
    ) = rest
    a = lax.axis_index("az")
    d = lax.axis_index("date")
    g = lax.axis_index("rg")
    lines = image.shape[2]
    samples = image.shape[3]
    loads = [
        pltpu.make_async_copy(source, target, load_sem.at[i])
        for i, (source, target) in enumerate(
            ((offsets_hbm, offsets), (taps_hbm, taps), (image_hbm, image), (table_hbm, table))
        )
    ]
    has_up = a > 0
    has_down = a < az_size - 1
    exists = {-1: has_up, 0: None, 1: has_down}

    def guarded(step, body):
        if exists[step] is None:
            body()
        else:
            pl.when(exists[step])(body)

    def place_at(az_step, date_step, other):
        return {
            "az": a + az_step,
            "date": lax.rem(d + date_step, date_size),
            "rg": 1 - g if other else g,
        }

    peers = [
        (o, t, k) for o in (-1, 0, 1) for t in range(date_size) for k in (0, 1)
        if (o, t, k) != (0, 0, 0)
    ]
    barrier = pltpu.get_barrier_semaphore()
    wraps = {t: d + t >= date_size for t in range(date_size)}

    def later(o, t, k, body):
        if o == 1:
            pl.when(has_down)(body)
        elif o == 0 and t == 0:
            body()
        elif o == 0:
            pl.when(jnp.logical_not(wraps[t]))(body)

    def earlier(o, t, k, body):
        if o == -1:
            pl.when(has_up)(body)
        elif o == 0 and t:
            pl.when(wraps[t])(body)

    for o, t, k in peers:
        later(o, t, k, lambda o=o, t=t, k=k: pl.semaphore_signal(
            barrier, inc=1, device_id=place_at(o, t, k), device_id_type=MESH))
    for load in loads:
        load.start()
    @pl.when(jnp.logical_not(has_up))
    def _():
        near[:, :, 0:REACH] = jnp.zeros((2, 2, REACH, samples), near.dtype)
        far[:, :, 0:REACH] = jnp.zeros((date_size - 1, 2, REACH, samples), far.dtype)
        near_side[0] = jnp.zeros(near_side.shape[1:], near_side.dtype)
        far_side[:, 0] = jnp.zeros((date_size - 1,) + far_side.shape[2:], far_side.dtype)
        all_kernels[:, 0] = jnp.zeros((date_size,) + all_kernels.shape[2:], jnp.float32)

    @pl.when(jnp.logical_not(has_down))
    def _():
        near[:, :, REACH + lines :] = jnp.zeros((2, 2, REACH, samples), near.dtype)
        far[:, :, REACH + lines :] = jnp.zeros((date_size - 1, 2, REACH, samples), far.dtype)
        near_side[2] = jnp.zeros(near_side.shape[1:], near_side.dtype)
        far_side[:, 2] = jnp.zeros((date_size - 1,) + far_side.shape[2:], far_side.dtype)
        all_kernels[:, 2] = jnp.zeros((date_size,) + all_kernels.shape[2:], jnp.float32)

    for load in loads[:3]:
        load.wait()
    shifts = jnp.broadcast_to(offsets[0:1, :].astype(jnp.float32), (TAPS, lines))
    held = jnp.concatenate([taps[:, 0], shifts], axis=1)
    kernels[...] = held
    all_kernels[0, 1] = held
    parts = ([], [])
    for c in range(2):
        value = image[c, 0]
        high = value.astype(jnp.bfloat16)
        low = (value - high.astype(jnp.float32)).astype(jnp.bfloat16)
        for i, piece in enumerate((high, low)):
            tile[i, c] = piece
            near[i, c, REACH : REACH + lines] = piece
            piece = piece.astype(jnp.float32)
            edge = jnp.where(g == 0, piece[:, samples - HALF :], piece[:, :HALF])
            parts[i].extend([edge[:HALF], edge[HALF:]])
    for i in range(2):
        pack[i] = jnp.concatenate(parts[i], axis=1).astype(jnp.bfloat16)

    pl.semaphore_wait(barrier, has_up.astype(jnp.int32) * (2 * date_size) + 2 * d + 1)
    for o, t, k in peers:
        earlier(o, t, k, lambda o=o, t=t, k=k: pl.semaphore_signal(
            ready.at[PLACE[-o], (date_size - t) % date_size, k], inc=1,
            device_id=place_at(o, t, k), device_id_type=MESH))

    taken = {
        1: (lines - REACH, REACH, 0), 0: (0, lines, REACH), -1: (0, REACH, REACH + lines),
    }

    def send(o, t, kind, target):
        slot = (date_size - t) % date_size
        spot = PLACE[o]
        first, size, land = taken[o]
        if kind == 0 and t == 0:
            src = tile.at[:, :, pl.ds(first, size), :]
            dst = near.at[:, :, pl.ds(land, size), :]
        elif kind == 0:
            src = tile.at[0, :, pl.ds(first, size), :]
            dst = far.at[slot - 1, :, pl.ds(land, size), :]
        elif kind == 1 and t == 0:
            src, dst = pack, near_side.at[spot]
        elif kind == 1:
            src, dst = pack.at[0], far_side.at[slot - 1, spot]
        else:
            src, dst = kernels, all_kernels.at[slot, spot]
        return pltpu.make_async_remote_copy(
            src_ref=src, dst_ref=dst,
            send_sem=send_sem.at[t, spot, kind],
            recv_sem=recv_sem.at[slot, spot, kind],
            device_id=target, device_id_type=MESH,
        )

    order = []
    for o, t, k in sorted(peers, key=lambda p: (p[0], p[1], p[2])):
        order += [(o, t, 1, 1)] if k else [(o, t, 2, 0), (o, t, 0, 0)]

    def push(o, t, k):
        for o2, t2, kind, k2 in order:
            if (o2, t2, k2) == (o, t, k):
                send(o, t, kind, place_at(o, t, k)).start()

    def answered(o, t, k):
        pl.semaphore_wait(ready.at[PLACE[o], t, k], 1)
        push(o, t, k)

    first = sorted(peers, key=lambda p: (p[0], p[1], p[2]))
    for o, t, k in first:
        if (o, t) == (0, 0):
            push(o, t, k)
        else:
            earlier(o, t, k, lambda o=o, t=t, k=k: push(o, t, k))
    for o, t, k in first:
        if (o, t) != (0, 0):
            later(o, t, k, lambda o=o, t=t, k=k: answered(o, t, k))

    def arrived(slot):
        for o, t, kind, k in order:
            if (date_size - t) % date_size == slot:
                guarded(-o, lambda o=o, t=t, kind=kind, k=k: send(
                    o, t, kind, place_at(-o, slot, k)).wait_recv())

    span = lines + 2 * REACH
    wide_lines = 4 * HALF
    source = lax.broadcasted_iota(jnp.int32, (span, wide_lines), 0)
    place = lax.broadcasted_iota(jnp.int32, (span, wide_lines), 1)
    distance = (source - place - (RIM - (TAPS // 2 - 1))).astype(jnp.float32)

    def resample(slot):
        above, own_rows, below = (all_kernels[slot, i] for i in range(3))
        weights = jnp.concatenate(
            [above[:, HALF:lines], own_rows[:, :lines], below[:, :HALF]], axis=1
        )
        shift = jnp.concatenate(
            [above[:, lines + HALF :], own_rows[:, lines:], below[:, lines : lines + HALF]], axis=1
        )
        gap = distance - shift[0:1]
        band = jnp.zeros((span, wide_lines), jnp.float32)
        for k in range(TAPS):
            band = jnp.where(gap == float(k), weights[k : k + 1], band)
        band_high = band.astype(jnp.bfloat16)
        band_low = (band - band_high.astype(jnp.float32)).astype(jnp.bfloat16)
        band_both = jnp.concatenate([band_high, band_low], axis=1)
        total = None
        for i in range(1 if slot else 2):
            columns = []
            for c in range(2):
                columns.append(far[slot - 1, c] if slot else near[i, c])
            blank = []
            for c in range(2):
                rows = []
                for spot in range(3):
                    value = far_side[slot - 1, spot] if slot else near_side[spot, i]
                    value = value.astype(jnp.float32)
                    first = 2 * c * HALF
                    both = jnp.concatenate(
                        [value[:, first : first + HALF], value[:, first + HALF : first + 2 * HALF]],
                        axis=0,
                    )
                    rows.append(
                        (both[lines - REACH :], both, both[:REACH])[spot]
                    )
                blank.append(jnp.concatenate(rows, axis=0))
            blank.append(jnp.zeros((span, 128 - 2 * HALF), jnp.float32))
            columns.append(jnp.concatenate(blank, axis=1).astype(jnp.bfloat16))
            product = lax.dot_general(
                jnp.concatenate(columns, axis=1), band_both, (((0,), (0,)), ((), ())),
                preferred_element_type=jnp.float32,
            )
            product = product[:, :wide_lines] + product[:, wide_lines:]
            total = product if total is None else total + product
        total = total.astype(jnp.bfloat16).astype(jnp.float32)
        core = jnp.concatenate([total[:samples], total[samples : 2 * samples]], axis=1)
        side = total[2 * samples : 2 * samples + 2 * HALF]
        side = jnp.concatenate([side[:HALF], side[HALF:]], axis=1)
        zero = jnp.zeros_like(side)
        turned[slot, 0:HALF] = jnp.where(g == 0, zero, side)
        turned[slot, HALF : HALF + samples] = core
        turned[slot, HALF + samples :] = jnp.where(g == 0, side, zero)

    def filtered(own, other):
        wide_lines = 2 * PATCH
        own_real, own_imag = own[:, :wide_lines], own[:, wide_lines:]
        other_real, other_imag = other[:, :wide_lines], other[:, wide_lines:]
        real_part = own_real * other_real + own_imag * other_imag
        imag_part = own_imag * other_real - own_real * other_imag
        ifg = jnp.concatenate([real_part, imag_part], axis=1).astype(jnp.bfloat16)
        spectra = jnp.dot(
            ifg, table[0 : 2 * wide_lines], preferred_element_type=jnp.float32
        ).astype(jnp.bfloat16)
        ring = table[4 * wide_lines :, 0:LANES]
        forward = table[4 * wide_lines : 5 * wide_lines, LANES : LANES + wide_lines]
        inverse = table[5 * wide_lines :, LANES : LANES + wide_lines]
        rows = [
            table[i * wide_lines : (i + 1) * wide_lines, LANES + wide_lines :].astype(jnp.float32)
            for i in (4, 5)
        ]
        weights = rows[0] + rows[1]
        weights = jnp.concatenate([weights] * (LANES // wide_lines), axis=1)
        columns = samples // HALF + 1
        for q in range(columns):
            rows = spectra[q * HALF : q * HALF + PATCH]
            block = jnp.concatenate([rows[:, :LANES], rows[:, LANES:]], axis=0)
            spectrum = jnp.dot(forward, block, preferred_element_type=jnp.float32)
            spec[q] = spectrum
            real, imag = spectrum[:PATCH], spectrum[PATCH:]
            power = real * real + imag * imag
            summed = power + pltpu.roll(power, 1, 0) + pltpu.roll(power, PATCH - 1, 0)
            power_sum[q * PATCH : (q + 1) * PATCH] = summed.astype(jnp.bfloat16)
        smooth = jnp.dot(power_sum[...], ring, preferred_element_type=jnp.float32)
        gains = lax.rsqrt(lax.rsqrt(1.0 + smooth * (1.0 / (9.0 * PATCH * PATCH))))
        for q in range(columns):
            gain = gains[q * PATCH : (q + 1) * PATCH]
            shaped[q, :PATCH] = (spec[q, :PATCH] * gain).astype(jnp.bfloat16)
            shaped[q, PATCH:] = (spec[q, PATCH:] * gain).astype(jnp.bfloat16)
        held = None
        for q in range(columns):
            ranged = jnp.dot(inverse, shaped[q], preferred_element_type=jnp.float32) * weights
            if held is not None:
                for c in range(2):
                    joined = held[c] + ranged[c * PATCH : c * PATCH + HALF]
                    back[(q - 1) * HALF : q * HALF, c * LANES : (c + 1) * LANES] = joined.astype(
                        jnp.bfloat16
                    )
            held = [ranged[c * PATCH + HALF : (c + 1) * PATCH] for c in range(2)]
        split = lax.dot_general(
            table[2 * wide_lines : 4 * wide_lines], back[...], (((1,), (1,)), ((), ())),
            preferred_element_type=jnp.float32,
        )
        return split[:wide_lines] + split[wide_lines:]

    arrived(0)
    resample(0)
    loads[3].wait()
    if count == date_size:
        for j in range(count):
            if j:
                arrived(j)
                resample(j)
            out[j] = filtered(turned[0], turned[j])
    else:
        for j in range(1, date_size):
            arrived(j)
            resample(j)
        for m in range(count):
            slot = lax.rem(matchings[d, m] - d + date_size, date_size)
            out[m] = filtered(turned[0], turned[slot])

    for o, t, kind, k in order:
        guarded(o, lambda o=o, t=t, kind=kind, k=k: send(
            o, t, kind, place_at(o, t, k)).wait_send())


def spread_kernel(date_size, count, matchings, results, out, sem):
    d = lax.axis_index("date")
    copies = []
    for m in range(out.shape[0]):
        spot = m
        if count == date_size:
            spot = lax.rem(matchings[d, m] - d + date_size, date_size)
        for c in range(2):
            copies.append(
                pltpu.make_async_copy(
                    results.at[spot, pl.ds(c * PATCH, PATCH)], out.at[m, c, 0], sem.at[m, c]
                )
            )
    for copy in copies:
        copy.start()
    for copy in copies:
        copy.wait()


def per_device(az_size, date_size, image_stack, tap_weights, offsets, matchings):
    lines, samples = image_stack.shape[2:]
    assert image_stack.shape[1] == 1 and lines == PATCH
    matches = matchings.shape[0]
    count = min(matches, date_size)
    columns = samples // HALF + 1
    by_date = matchings.T
    hbm = pl.BlockSpec(memory_space=pltpu.HBM)
    vmem = pl.BlockSpec(memory_space=pltpu.VMEM)
    smem = pl.BlockSpec(memory_space=pltpu.SMEM)
    constants = tables()
    extra = [by_date] if count < date_size else []
    results = pl.pallas_call(
        functools.partial(stack_kernel, az_size, date_size, count),
        out_shape=pltpu.VMEM((count, 2 * lines, samples), jnp.float32),
        in_specs=[hbm] * 4 + [smem] * len(extra),
        out_specs=vmem,
        scratch_shapes=[
            pltpu.VMEM(image_stack.shape, jnp.float32),
            pltpu.VMEM(tap_weights.shape, jnp.float32),
            pltpu.VMEM(offsets.shape, jnp.int32),
            pltpu.VMEM(constants.shape, jnp.bfloat16),
            pltpu.VMEM((2, 2, lines, samples), jnp.bfloat16),
            pltpu.VMEM((2, HALF, 4 * HALF), jnp.bfloat16),
            pltpu.VMEM((TAPS, 2 * lines), jnp.float32),
            pltpu.VMEM((2, 2, lines + 2 * REACH, samples), jnp.bfloat16),
            pltpu.VMEM((date_size - 1, 2, lines + 2 * REACH, samples), jnp.bfloat16),
            pltpu.VMEM((3, 2, HALF, 4 * HALF), jnp.bfloat16),
            pltpu.VMEM((date_size - 1, 3, HALF, 4 * HALF), jnp.bfloat16),
            pltpu.VMEM((date_size, 3, TAPS, 2 * lines), jnp.float32),
            pltpu.VMEM((date_size, samples + 2 * HALF, 8 * HALF), jnp.float32),
            pltpu.VMEM((columns, 2 * PATCH, LANES), jnp.float32),
            pltpu.VMEM((columns * PATCH, LANES), jnp.bfloat16),
            pltpu.VMEM((columns, 2 * PATCH, LANES), jnp.bfloat16),
            pltpu.VMEM((samples, 2 * LANES), jnp.bfloat16),
            pltpu.SemaphoreType.DMA((4,)),
            pltpu.SemaphoreType.DMA((date_size, 3, 3)),
            pltpu.SemaphoreType.DMA((date_size, 3, 3)),
            pltpu.SemaphoreType.REGULAR((3, date_size, 2)),
        ],
        compiler_params=pltpu.CompilerParams(collective_id=0, has_side_effects=True),
    )(image_stack, tap_weights, offsets, jnp.asarray(constants), *extra)
    return pl.pallas_call(
        functools.partial(spread_kernel, date_size, count),
        out_shape=jax.ShapeDtypeStruct((matches, 2, 1, lines, samples), jnp.float32),
        in_specs=[smem, vmem],
        out_specs=hbm,
        scratch_shapes=[pltpu.SemaphoreType.DMA((matches, 2))],
        compiler_params=pltpu.CompilerParams(vmem_limit_bytes=16 << 20),
    )(by_date, results)


def solution(mesh):
    placed = (
        P(None, ("parts", "date"), "az", "rg"),
        P(None, ("parts", "date"), "az"),
        P(("parts", "date"), "az"),
        P(),
    )
    assert mesh.shape["rg"] == 2
    return jax.shard_map(
        functools.partial(per_device, mesh.shape["az"], mesh.shape["date"]),
        mesh=mesh,
        in_specs=placed,
        out_specs=P(None, None, ("parts", "date"), "az", "rg"),
        check_vma=False,
    )
```

```python
import functools
import math

import jax
import jax.numpy as jnp
import ml_dtypes
import numpy as np
from jax import lax
from jax.experimental import pallas as pl
from jax.experimental.pallas import tpu as pltpu
from jax.sharding import PartitionSpec as P

TAPS = 8
SHIFT_MAX = 12
PATCH = 64
HALF = PATCH // 2
RIM = SHIFT_MAX + TAPS // 2
REACH = RIM + HALF
GROUPS = 4
LANES = GROUPS * PATCH
HALF_LANES = 128
HALF_GROUP = HALF + 3
MESH = pl.DeviceIdType.MESH
BF16 = ml_dtypes.bfloat16
PLACE = {1: 0, 0: 1, -1: 2}


def fourier_table(sine_sign, table_scale):
    ids = np.arange(PATCH)
    angles = ((ids[:, None] * ids[None, :]) % PATCH) * (2.0 * math.pi / PATCH)
    cosine = np.cos(angles) * table_scale
    sine = np.sin(angles) * (sine_sign * table_scale)
    table = np.block([[cosine, -sine], [sine, cosine]]).astype(np.float32)
    return table.astype(BF16).astype(np.float32)


def tables():
    forward = fourier_table(1.0, 1.0)
    inverse = fourier_table(-1.0, 1.0 / PATCH)
    window = np.sin(math.pi * (np.arange(PATCH, dtype=np.float32) + 0.5) / PATCH) ** 2
    wide = 2 * PATCH
    line_in = np.zeros((2, wide, 2, GROUPS, PATCH), np.float32)
    line_out = np.zeros((2, PATCH, 2, GROUPS, PATCH), np.float32)
    real_in = np.zeros((wide, 2, HALF_LANES), np.float32)
    real_out = np.zeros((PATCH, 2, HALF_LANES), np.float32)
    real_ring = np.zeros((HALF_LANES, HALF_LANES), np.float32)
    split_f = forward.reshape(2, PATCH, 2, PATCH)
    split_i = inverse.reshape(2, PATCH, 2, PATCH)
    for r in range(3):
        line_in[:, r * HALF : r * HALF + PATCH, :, r] = split_f
        for at in range(HALF_GROUP):
            f, lane = (at - 1) % PATCH, r * HALF_GROUP + at
            real_in[r * HALF : r * HALF + PATCH, :, lane] = split_f[0, :, :, f]
            if 0 < at < HALF_GROUP - 1:
                real_ring[lane - 1 : lane + 2, lane] = 1.0
        for line in range(PATCH):
            u = line + HALF - HALF * r
            if 0 <= u < PATCH:
                line_out[:, line, :, r] = split_i[:, :, :, u].transpose(2, 0, 1) * window[u]
                for at in range(1, HALF_GROUP - 1):
                    f = at - 1
                    times = 1.0 if f in (0, HALF) else 2.0
                    real_out[line, :, r * HALF_GROUP + at] = split_i[:, f, 0, u] * window[u] * times
    line_in = line_in.reshape(2 * wide, 2 * LANES).astype(BF16)
    line_out = line_out.reshape(wide, 2 * LANES)
    high = line_out.astype(BF16)
    low = (line_out - high.astype(np.float32)).astype(BF16)
    ids = np.arange(LANES)
    gap = (ids[:, None] - ids[None, :]) % PATCH
    same = ids[:, None] // PATCH == ids[None, :] // PATCH
    ring = (((gap <= 1) | (gap == PATCH - 1)) & same).astype(BF16)
    turns = np.concatenate([forward.T, inverse.T], axis=0).astype(BF16)
    rows = np.broadcast_to(np.tile(window, 2)[:, None], (wide, wide)).astype(np.float32)
    rows_high = rows.astype(BF16)
    rows_low = (rows - rows_high.astype(np.float32)).astype(BF16)
    last = np.concatenate([ring, turns, np.concatenate([rows_high, rows_low], axis=0)], axis=1)
    real_in = real_in.reshape(wide, 2 * HALF_LANES).astype(BF16)
    real_out = real_out.reshape(PATCH, 2 * HALF_LANES)
    real_high = real_out.astype(BF16)
    real_low = (real_out - real_high.astype(np.float32)).astype(BF16)
    real = np.concatenate([real_in, np.concatenate([real_high, real_low], axis=0)], axis=1)
    rest = np.zeros((wide, 2 * LANES), BF16)
    rest[:, :HALF_LANES] = real_ring.astype(BF16)
    return np.concatenate([line_in, high, low, last, real, rest], axis=0)


def filter_patches(ifg, table, spec, power_sum, shaped, back, real):
    wide = 2 * PATCH
    rows, depth = ifg.shape[0], (1 if real else 2) * wide
    lanes = HALF_LANES if real else LANES
    columns = rows // HALF - 1
    line_in = table[6 * wide : 7 * wide, 0:LANES] if real else table[0 : 2 * wide]
    ring = table[7 * wide :, 0:lanes] if real else table[4 * wide : 6 * wide, 0:LANES]
    line_out = table[6 * wide : 7 * wide, LANES:] if real else table[2 * wide : 4 * wide]
    forward = table[4 * wide : 5 * wide, LANES : LANES + wide]
    inverse = table[5 * wide : 6 * wide, LANES : LANES + wide]
    pieces = [
        table[i * wide : (i + 1) * wide, LANES + wide : LANES + 2 * wide].astype(jnp.float32)
        for i in (4, 5)
    ]
    weights = jnp.concatenate([pieces[0] + pieces[1]] * (lanes // wide), axis=1)
    spectra = jnp.dot(
        ifg[:, :depth], line_in, preferred_element_type=jnp.float32
    ).astype(jnp.bfloat16)
    for q in range(columns):
        block = spectra[q * HALF : q * HALF + PATCH]
        block = jnp.concatenate([block[:, :lanes], block[:, lanes:]], axis=0)
        spectrum = jnp.dot(forward, block, preferred_element_type=jnp.float32)
        spec[q, :, :lanes] = spectrum
        re, im = spectrum[:PATCH], spectrum[PATCH:]
        power = re * re + im * im
        summed = power + pltpu.roll(power, 1, 0) + pltpu.roll(power, PATCH - 1, 0)
        power_sum[q * PATCH : (q + 1) * PATCH, :lanes] = summed.astype(jnp.bfloat16)
    smooth = jnp.dot(power_sum[:, :lanes], ring, preferred_element_type=jnp.float32)
    gains = lax.rsqrt(lax.rsqrt(1.0 + smooth * (1.0 / (9.0 * PATCH * PATCH))))
    for q in range(columns):
        gain = gains[q * PATCH : (q + 1) * PATCH]
        shaped[q, :PATCH, :lanes] = (spec[q, :PATCH, :lanes] * gain).astype(jnp.bfloat16)
        shaped[q, PATCH:, :lanes] = (spec[q, PATCH:, :lanes] * gain).astype(jnp.bfloat16)
    held = None
    for q in range(columns):
        ranged = jnp.dot(
            inverse, shaped[q, :, :lanes], preferred_element_type=jnp.float32) * weights
        if held is not None:
            for c in range(2):
                joined = held[c] + ranged[c * PATCH : c * PATCH + HALF]
                back[(q - 1) * HALF : q * HALF, c * lanes : (c + 1) * lanes] = joined.astype(
                    jnp.bfloat16
                )
        held = [ranged[c * PATCH + HALF : (c + 1) * PATCH] for c in range(2)]
    split = lax.dot_general(
        line_out, back[:, : 2 * lanes], (((1,), (1,)), ((), ())),
        preferred_element_type=jnp.float32,
    )
    tall = split.shape[0] // 2
    return split[:tall] + split[tall:]


def scratch_of_filter(samples, lanes):
    columns = samples // HALF + 1
    return [
        pltpu.VMEM((columns, 2 * PATCH, lanes), jnp.float32),
        pltpu.VMEM((columns * PATCH, lanes), jnp.bfloat16),
        pltpu.VMEM((columns, 2 * PATCH, lanes), jnp.bfloat16),
        pltpu.VMEM((samples, 2 * lanes), jnp.bfloat16),
    ]


def stack_kernel(
    az_size, date_size, image_hbm, taps_hbm, offsets_hbm, table_hbm, ifg, table, *rest,
):
    alone = spec = power_sum = shaped = back = None
    if date_size == 2:
        alone, *rest = rest
        spec, power_sum, shaped, back, *rest = rest
    (
        image, taps, offsets, tile, kernels, near, far, margin, all_kernels, own,
        load_sem, send_sem, recv_sem, side_sem, ready,
    ) = rest
    a = lax.axis_index("az")
    d = lax.axis_index("date")
    g = lax.axis_index("rg")
    lines = image.shape[2]
    samples = image.shape[3]
    wide = 2 * PATCH
    loads = [
        pltpu.make_async_copy(source, target, load_sem.at[i])
        for i, (source, target) in enumerate(
            ((offsets_hbm, offsets), (taps_hbm, taps), (image_hbm, image), (table_hbm, table))
        )
    ]
    has_up = a > 0
    has_down = a < az_size - 1
    exists = {-1: has_up, 0: None, 1: has_down}
    wraps = {t: d + t >= date_size for t in range(date_size)}

    def guarded(step, body):
        if exists[step] is None:
            body()
        else:
            pl.when(exists[step])(body)

    def place_at(az_step, date_step):
        return {"az": a + az_step, "date": lax.rem(d + date_step, date_size), "rg": g}

    other_core = {"az": a, "date": d, "rg": 1 - g}
    peers = [(o, t) for o in (-1, 0, 1) for t in range(date_size) if (o, t) != (0, 0)]

    barrier = pltpu.get_barrier_semaphore()
    pl.semaphore_signal(barrier, inc=1, device_id=other_core, device_id_type=MESH)
    for o, t in peers:
        if o >= 0:
            @pl.when(jnp.logical_and(jnp.logical_not(wraps[t]), has_down if o else True))
            def _(o=o, t=t):
                pl.semaphore_signal(barrier, inc=1, device_id=place_at(o, t), device_id_type=MESH)
    for load in loads[:3]:
        load.start()

    @pl.when(jnp.logical_not(has_up))
    def _():
        margin[0] = jnp.zeros(margin.shape[1:], margin.dtype)
        far[:, :, 0:REACH] = jnp.zeros((date_size - 1, 2, REACH, samples), far.dtype)
        all_kernels[:, 0] = jnp.zeros((date_size,) + all_kernels.shape[2:], jnp.float32)

    @pl.when(jnp.logical_not(has_down))
    def _():
        margin[1] = jnp.zeros(margin.shape[1:], margin.dtype)
        far[:, :, REACH + lines :] = jnp.zeros((date_size - 1, 2, REACH, samples), far.dtype)
        all_kernels[:, 2] = jnp.zeros((date_size,) + all_kernels.shape[2:], jnp.float32)

    no_side = jnp.zeros((date_size, HALF, ifg.shape[2]), ifg.dtype)

    @pl.when(g == 0)
    def _():
        ifg[:, 0:HALF] = no_side

    @pl.when(g != 0)
    def _():
        ifg[:, HALF + samples :] = no_side

    taken = {
        1: (lines - REACH, REACH, 0), 0: (0, lines, REACH), -1: (0, REACH, REACH + lines),
    }

    def send(o, t, kind, target):
        slot = (date_size - t) % date_size
        spot = PLACE[o]
        first, size, land = taken[o]
        if kind == 0 and t == 0:
            src = image_hbm.at[:, 0, pl.ds(first, size), :]
            dst = margin.at[0 if o == 1 else 1]
        elif kind == 0:
            src = tile.at[:, pl.ds(first, size), :]
            dst = far.at[slot - 1, :, pl.ds(land, size), :]
        else:
            src, dst = kernels, all_kernels.at[slot, spot]
        return pltpu.make_async_remote_copy(
            src_ref=src, dst_ref=dst,
            send_sem=send_sem.at[t, spot, kind],
            recv_sem=recv_sem.at[slot, spot, kind],
            device_id=target, device_id_type=MESH,
        )

    def push(o, t, kind):
        send(o, t, kind, place_at(o, t)).start()

    pl.semaphore_wait(barrier, has_up.astype(jnp.int32) * (d + 1) + d + 1)
    for o, t in peers:
        if o <= 0:
            @pl.when(jnp.logical_and(wraps[t] if t else True, has_up if o else True))
            def _(o=o, t=t):
                pl.semaphore_signal(
                    ready.at[PLACE[-o], (date_size - t) % date_size], inc=1,
                    device_id=place_at(o, t), device_id_type=MESH)

    leads = d == 0

    @pl.when(jnp.logical_and(has_up, leads))
    def _():
        push(-1, 0, 0)

    for load in loads[:2]:
        load.wait()
    shifts = jnp.broadcast_to(offsets[0:1, :].astype(jnp.float32), (TAPS, lines))
    held = jnp.concatenate([taps[:, 0], shifts], axis=1)
    kernels[...] = held
    all_kernels[0, 1] = held

    @pl.when(jnp.logical_and(has_up, leads))
    def _():
        push(-1, 0, 1)

    loads[2].wait()
    for c in range(2):
        tile[c] = image[c, 0].astype(jnp.bfloat16)
    for t in range(1, date_size):
        @pl.when(wraps[t])
        def _(t=t):
            @pl.when(has_up)
            def _():
                push(-1, t, 1)
                push(-1, t, 0)

            push(0, t, 1)
            push(0, t, 0)

    @pl.when(jnp.logical_and(has_up, jnp.logical_not(leads)))
    def _():
        push(-1, 0, 1)
        push(-1, 0, 0)

    loads[3].start()
    for c in range(2):
        value = image[c, 0]
        high = value.astype(jnp.bfloat16)
        near[0, c, REACH : REACH + lines] = high
        near[1, c, REACH : REACH + lines] = (value - high.astype(jnp.float32)).astype(jnp.bfloat16)

    for t in range(1, date_size):
        @pl.when(jnp.logical_not(wraps[t]))
        def _(t=t):
            pl.semaphore_wait(ready.at[PLACE[0], t], 1)
            push(0, t, 1)
            push(0, t, 0)

            @pl.when(has_up)
            def _():
                push(-1, t, 1)
                push(-1, t, 0)

    @pl.when(has_down)
    def _():
        pl.semaphore_wait(ready.at[PLACE[1], 0], 1)
        for t in range(1, date_size):
            @pl.when(wraps[t])
            def _(t=t):
                push(1, t, 1)
                push(1, t, 0)

        push(1, 0, 1)
        push(1, 0, 0)
        for t in range(1, date_size):
            @pl.when(jnp.logical_not(wraps[t]))
            def _(t=t):
                pl.semaphore_wait(ready.at[PLACE[1], t], 1)
                push(1, t, 1)
                push(1, t, 0)

    def arrived(slot):
        t = (date_size - slot) % date_size
        for o in (-1, 0, 1):
            if (o, t) != (0, 0):
                def _(o=o):
                    for kind in (1, 0):
                        send(o, t, kind, place_at(-o, slot)).wait_recv()
                guarded(-o, _)

    def side(slot):
        return pltpu.make_async_remote_copy(
            src_ref=ifg.at[slot, pl.ds(pl.multiple_of(samples - (samples - HALF) * g, HALF), HALF)],
            dst_ref=ifg.at[slot, pl.ds(pl.multiple_of((samples + HALF) * g, HALF), HALF)],
            send_sem=side_sem.at[0, slot], recv_sem=side_sem.at[1, slot],
            device_id=other_core, device_id_type=MESH,
        )

    def side_arrived(slot):
        pltpu.make_async_remote_copy(
            src_ref=ifg.at[slot, pl.ds(pl.multiple_of(samples - (samples - HALF) * g, HALF), HALF)],
            dst_ref=ifg.at[slot, pl.ds(pl.multiple_of((samples + HALF) * (1 - g), HALF), HALF)],
            send_sem=side_sem.at[0, slot], recv_sem=side_sem.at[1, slot],
            device_id=other_core, device_id_type=MESH,
        ).wait_recv()

    span = lines + 2 * REACH
    wide_lines = 4 * HALF
    source = lax.broadcasted_iota(jnp.int32, (span, wide_lines), 0)
    place = lax.broadcasted_iota(jnp.int32, (span, wide_lines), 1)
    distance = (source - place - (RIM - (TAPS // 2 - 1))).astype(jnp.float32)

    def resample(slot):
        above, own_rows, below = (all_kernels[slot, i] for i in range(3))
        weights = jnp.concatenate(
            [above[:, HALF:lines], own_rows[:, :lines], below[:, :HALF]], axis=1
        )
        shift = jnp.concatenate(
            [above[:, lines + HALF :], own_rows[:, lines:], below[:, lines : lines + HALF]], axis=1
        )
        gap = distance - shift[0:1]
        band = jnp.zeros((span, wide_lines), jnp.float32)
        for k in range(TAPS):
            band = jnp.where(gap == float(k), weights[k : k + 1], band)
        band_high = band.astype(jnp.bfloat16)
        band_low = (band - band_high.astype(jnp.float32)).astype(jnp.bfloat16)
        band_both = jnp.concatenate([band_high, band_low], axis=1)
        total = None
        for i in range(1 if slot else 2):
            columns = [far[slot - 1, c] if slot else near[i, c] for c in range(2)]
            product = lax.dot_general(
                jnp.concatenate(columns, axis=1), band_both, (((0,), (0,)), ((), ())),
                preferred_element_type=jnp.float32,
            )
            product = product[:, :wide_lines] + product[:, wide_lines:]
            total = product if total is None else total + product
        total = total.astype(jnp.bfloat16).astype(jnp.float32)
        return total[:samples], total[samples:]

    def combine(slot):
        if slot == 0:
            for i in range(2):
                for c in range(2):
                    value = margin[i, c]
                    high = value.astype(jnp.bfloat16)
                    at = slice(0, REACH) if i == 0 else slice(REACH + lines, span)
                    near[0, c, at] = high
                    near[1, c, at] = (value - high.astype(jnp.float32)).astype(jnp.bfloat16)
        real, imag = resample(slot)
        if slot == 0:
            own[0], own[1] = real, imag
            real_part, imag_part = real * real + imag * imag, jnp.zeros_like(real)
        else:
            real_part = own[0] * real + own[1] * imag
            imag_part = own[1] * real - own[0] * imag
        ifg[slot, HALF : HALF + samples, :wide_lines] = real_part.astype(jnp.bfloat16)
        ifg[slot, HALF : HALF + samples, wide_lines:] = imag_part.astype(jnp.bfloat16)
        side(slot).start()

    arrived(0)
    combine(0)
    for j in range(1, date_size):
        arrived(j)
        combine(j)
    loads[3].wait()
    side_arrived(0)
    if alone is not None:
        alone[...] = filter_patches(ifg.at[0], table, spec, power_sum, shaped, back, True)
    for j in range(1, date_size):
        side_arrived(j)

    for o, t in peers:
        def _(o=o, t=t):
            for kind in (1, 0):
                send(o, t, kind, place_at(o, t)).wait_send()
        guarded(o, _)
    for slot in range(date_size):
        side(slot).wait_send()


def filter_kernel(date_size, by_date, ifg, table, *rest):
    alone = None
    if date_size == 2:
        alone, *rest = rest
    out, results, blank, partner, spec, power_sum, shaped, back, sem, read_sem = rest
    matches = out.shape[0]
    d = lax.axis_index("date")
    read = pltpu.make_async_copy(by_date, partner, read_sem)
    read.start()

    def deliver(m, c, source):
        return pltpu.make_async_copy(source, out.at[m, c, 0], sem.at[m, c])

    if alone is not None:
        blank[...] = jnp.zeros(blank.shape, blank.dtype)
        results[0] = filter_patches(ifg.at[1], table, spec, power_sum, shaped, back, False)
        read.wait()
        for m in range(matches):
            @pl.when(partner[d, m] == d)
            def _(m=m):
                deliver(m, 0, alone).start()
                deliver(m, 1, blank).start()

            @pl.when(partner[d, m] != d)
            def _(m=m):
                for c in range(2):
                    deliver(m, c, results.at[0, pl.ds(c * PATCH, PATCH)]).start()
    else:
        read.wait()
        for m in range(matches):
            slot = lax.rem(partner[d, m] - d + date_size, date_size)
            results[m] = filter_patches(
                ifg.at[slot], table, spec, power_sum, shaped, back, False)
            for c in range(2):
                deliver(m, c, results.at[m, pl.ds(c * PATCH, PATCH)]).start()
    for m in range(matches):
        for c in range(2):
            deliver(m, c, results.at[0, pl.ds(c * PATCH, PATCH)]).wait()


def per_device(az_size, date_size, image_stack, tap_weights, offsets, matchings):
    lines, samples = image_stack.shape[2:]
    assert image_stack.shape[1] == 1 and lines == PATCH
    matches = matchings.shape[0]
    hbm = pl.BlockSpec(memory_space=pltpu.HBM)
    vmem = pl.BlockSpec(memory_space=pltpu.VMEM)
    constants = tables()
    alone = date_size == 2
    passed = [
        pltpu.VMEM((date_size, samples + 2 * HALF, 8 * HALF), jnp.bfloat16),
        pltpu.VMEM(constants.shape, jnp.bfloat16),
    ]
    if alone:
        passed.append(pltpu.VMEM((lines, samples), jnp.float32))
    passed = pl.pallas_call(
        functools.partial(stack_kernel, az_size, date_size),
        out_shape=passed,
        in_specs=[hbm] * 4,
        out_specs=[vmem] * len(passed),
        scratch_shapes=(scratch_of_filter(samples, HALF_LANES) if alone else []) + [
            pltpu.VMEM(image_stack.shape, jnp.float32),
            pltpu.VMEM(tap_weights.shape, jnp.float32),
            pltpu.VMEM(offsets.shape, jnp.int32),
            pltpu.VMEM((2, lines, samples), jnp.bfloat16),
            pltpu.VMEM((TAPS, 2 * lines), jnp.float32),
            pltpu.VMEM((2, 2, lines + 2 * REACH, samples), jnp.bfloat16),
            pltpu.VMEM((date_size - 1, 2, lines + 2 * REACH, samples), jnp.bfloat16),
            pltpu.VMEM((2, 2, REACH, samples), jnp.float32),
            pltpu.VMEM((date_size, 3, TAPS, 2 * lines), jnp.float32),
            pltpu.VMEM((2, samples, 4 * HALF), jnp.float32),
            pltpu.SemaphoreType.DMA((4,)),
            pltpu.SemaphoreType.DMA((date_size, 3, 2)),
            pltpu.SemaphoreType.DMA((date_size, 3, 2)),
            pltpu.SemaphoreType.DMA((2, date_size)),
            pltpu.SemaphoreType.REGULAR((3, date_size)),
        ],
        compiler_params=pltpu.CompilerParams(collective_id=0, has_side_effects=True),
    )(image_stack, tap_weights, offsets, jnp.asarray(constants))
    return pl.pallas_call(
        functools.partial(filter_kernel, date_size),
        out_shape=jax.ShapeDtypeStruct((matches, 2, 1, lines, samples), jnp.float32),
        in_specs=[hbm] + [vmem] * len(passed),
        out_specs=hbm,
        scratch_shapes=[
            pltpu.VMEM((1 if alone else matches, 2 * lines, samples), jnp.float32),
            pltpu.VMEM((lines, samples), jnp.float32),
            pltpu.SMEM((date_size, matches), jnp.int32),
        ] + scratch_of_filter(samples, LANES) + [
            pltpu.SemaphoreType.DMA((matches, 2)),
            pltpu.SemaphoreType.DMA,
        ],
        compiler_params=pltpu.CompilerParams(vmem_limit_bytes=24 << 20),
    )(matchings.T, *passed)


def solution(mesh):
    placed = (
        P(None, ("parts", "date"), "az", "rg"),
        P(None, ("parts", "date"), "az"),
        P(("parts", "date"), "az"),
        P(),
    )
    assert mesh.shape["rg"] == 2
    return jax.shard_map(
        functools.partial(per_device, mesh.shape["az"], mesh.shape["date"]),
        mesh=mesh,
        in_specs=placed,
        out_specs=P(None, None, ("parts", "date"), "az", "rg"),
        check_vma=False,
    )
```

```python
import functools
import math

import jax
import jax.numpy as jnp
import ml_dtypes
import numpy as np
from jax import lax
from jax.experimental import pallas as pl
from jax.experimental.pallas import tpu as pltpu
from jax.sharding import PartitionSpec as P

TAPS = 8
SHIFT_MAX = 12
PATCH = 64
HALF = PATCH // 2
RIM = SHIFT_MAX + TAPS // 2
REACH = RIM + HALF
GROUPS = 4
LANES = GROUPS * PATCH
HALF_LANES = 128
HALF_GROUP = HALF + 3
MESH = pl.DeviceIdType.MESH
BF16 = ml_dtypes.bfloat16
PLACE = {1: 0, 0: 1, -1: 2}


def fourier_table(sine_sign, table_scale):
    ids = np.arange(PATCH)
    angles = ((ids[:, None] * ids[None, :]) % PATCH) * (2.0 * math.pi / PATCH)
    cosine = np.cos(angles) * table_scale
    sine = np.sin(angles) * (sine_sign * table_scale)
    table = np.block([[cosine, -sine], [sine, cosine]]).astype(np.float32)
    return table.astype(BF16).astype(np.float32)


def tables():
    forward = fourier_table(1.0, 1.0)
    inverse = fourier_table(-1.0, 1.0 / PATCH)
    window = np.sin(math.pi * (np.arange(PATCH, dtype=np.float32) + 0.5) / PATCH) ** 2
    wide = 2 * PATCH
    line_in = np.zeros((2, wide, 2, GROUPS, PATCH), np.float32)
    line_out = np.zeros((2, PATCH, 2, GROUPS, PATCH), np.float32)
    real_in = np.zeros((wide, 2, HALF_LANES), np.float32)
    real_out = np.zeros((PATCH, 2, HALF_LANES), np.float32)
    real_ring = np.zeros((HALF_LANES, HALF_LANES), np.float32)
    split_f = forward.reshape(2, PATCH, 2, PATCH)
    split_i = inverse.reshape(2, PATCH, 2, PATCH)
    for r in range(3):
        line_in[:, r * HALF : r * HALF + PATCH, :, r] = split_f
        for at in range(HALF_GROUP):
            f, lane = (at - 1) % PATCH, r * HALF_GROUP + at
            real_in[r * HALF : r * HALF + PATCH, :, lane] = split_f[0, :, :, f]
            if 0 < at < HALF_GROUP - 1:
                real_ring[lane - 1 : lane + 2, lane] = 1.0
        for line in range(PATCH):
            u = line + HALF - HALF * r
            if 0 <= u < PATCH:
                line_out[:, line, :, r] = split_i[:, :, :, u].transpose(2, 0, 1) * window[u]
                for at in range(1, HALF_GROUP - 1):
                    f = at - 1
                    times = 1.0 if f in (0, HALF) else 2.0
                    real_out[line, :, r * HALF_GROUP + at] = split_i[:, f, 0, u] * window[u] * times
    line_in = line_in.reshape(2 * wide, 2 * LANES).astype(BF16)
    line_out = line_out.reshape(wide, 2 * LANES)
    high = line_out.astype(BF16)
    low = (line_out - high.astype(np.float32)).astype(BF16)
    ids = np.arange(LANES)
    gap = (ids[:, None] - ids[None, :]) % PATCH
    same = ids[:, None] // PATCH == ids[None, :] // PATCH
    ring = (((gap <= 1) | (gap == PATCH - 1)) & same).astype(BF16)
    turns = np.concatenate([forward.T, inverse.T], axis=0).astype(BF16)
    rows = np.broadcast_to(np.tile(window, 2)[:, None], (wide, wide)).astype(np.float32)
    rows_high = rows.astype(BF16)
    rows_low = (rows - rows_high.astype(np.float32)).astype(BF16)
    last = np.concatenate([ring, turns, np.concatenate([rows_high, rows_low], axis=0)], axis=1)
    real_in = real_in.reshape(wide, 2 * HALF_LANES).astype(BF16)
    real_out = real_out.reshape(PATCH, 2 * HALF_LANES)
    real_high = real_out.astype(BF16)
    real_low = (real_out - real_high.astype(np.float32)).astype(BF16)
    real = np.concatenate([real_in, np.concatenate([real_high, real_low], axis=0)], axis=1)
    rest = np.zeros((wide, 2 * LANES), BF16)
    rest[:, :HALF_LANES] = real_ring.astype(BF16)
    return np.concatenate([line_in, high, low, last, real, rest], axis=0)


def filter_patches(ifg, table, spec, power_sum, shaped, back, real):
    wide = 2 * PATCH
    rows, depth = ifg.shape[0], (1 if real else 2) * wide
    lanes = HALF_LANES if real else LANES
    columns = rows // HALF - 1
    line_in = table[6 * wide : 7 * wide, 0:LANES] if real else table[0 : 2 * wide]
    ring = table[7 * wide :, 0:lanes] if real else table[4 * wide : 6 * wide, 0:LANES]
    line_out = table[6 * wide : 7 * wide, LANES:] if real else table[2 * wide : 4 * wide]
    forward = table[4 * wide : 5 * wide, LANES : LANES + wide]
    inverse = table[5 * wide : 6 * wide, LANES : LANES + wide]
    pieces = [
        table[i * wide : (i + 1) * wide, LANES + wide : LANES + 2 * wide].astype(jnp.float32)
        for i in (4, 5)
    ]
    weights = jnp.concatenate([pieces[0] + pieces[1]] * (lanes // wide), axis=1)
    spectra = jnp.dot(
        ifg[:, :depth], line_in, preferred_element_type=jnp.float32
    ).astype(jnp.bfloat16)
    for q in range(columns):
        block = spectra[q * HALF : q * HALF + PATCH]
        block = jnp.concatenate([block[:, :lanes], block[:, lanes:]], axis=0)
        spectrum = jnp.dot(forward, block, preferred_element_type=jnp.float32)
        spec[q, :, :lanes] = spectrum
        re, im = spectrum[:PATCH], spectrum[PATCH:]
        power = re * re + im * im
        summed = power + pltpu.roll(power, 1, 0) + pltpu.roll(power, PATCH - 1, 0)
        power_sum[q * PATCH : (q + 1) * PATCH, :lanes] = summed.astype(jnp.bfloat16)
    smooth = jnp.dot(power_sum[:, :lanes], ring, preferred_element_type=jnp.float32)
    gains = lax.rsqrt(lax.rsqrt(1.0 + smooth * (1.0 / (9.0 * PATCH * PATCH))))
    for q in range(columns):
        gain = gains[q * PATCH : (q + 1) * PATCH]
        shaped[q, :PATCH, :lanes] = (spec[q, :PATCH, :lanes] * gain).astype(jnp.bfloat16)
        shaped[q, PATCH:, :lanes] = (spec[q, PATCH:, :lanes] * gain).astype(jnp.bfloat16)
    held = None
    for q in range(columns):
        ranged = jnp.dot(
            inverse, shaped[q, :, :lanes], preferred_element_type=jnp.float32) * weights
        if held is not None:
            for c in range(2):
                joined = held[c] + ranged[c * PATCH : c * PATCH + HALF]
                back[(q - 1) * HALF : q * HALF, c * lanes : (c + 1) * lanes] = joined.astype(
                    jnp.bfloat16
                )
        held = [ranged[c * PATCH + HALF : (c + 1) * PATCH] for c in range(2)]
    split = lax.dot_general(
        line_out, back[:, : 2 * lanes], (((1,), (1,)), ((), ())),
        preferred_element_type=jnp.float32,
    )
    tall = split.shape[0] // 2
    return split[:tall] + split[tall:]


def scratch_of_filter(samples, lanes):
    columns = samples // HALF + 1
    return [
        pltpu.VMEM((columns, 2 * PATCH, lanes), jnp.float32),
        pltpu.VMEM((columns * PATCH, lanes), jnp.bfloat16),
        pltpu.VMEM((columns, 2 * PATCH, lanes), jnp.bfloat16),
        pltpu.VMEM((samples, 2 * lanes), jnp.bfloat16),
    ]


def stack_kernel(
    az_size, date_size, image_hbm, taps_hbm, offsets_hbm, table_hbm, by_date, ifg, table, passed,
    *rest,
):
    alone = spec = power_sum = shaped = back = None
    if date_size == 2:
        alone, *rest = rest
        spec, power_sum, shaped, back, *rest = rest
    (
        image, taps, offsets, tile, kernels, near, far, margin, all_kernels, own,
        load_sem, send_sem, recv_sem, side_sem, ready,
    ) = rest
    a = lax.axis_index("az")
    d = lax.axis_index("date")
    g = lax.axis_index("rg")
    lines = image.shape[2]
    samples = image.shape[3]
    wide = 2 * PATCH
    loads = [
        pltpu.make_async_copy(source, target, load_sem.at[i])
        for i, (source, target) in enumerate(
            ((offsets_hbm, offsets), (taps_hbm, taps), (image_hbm, image), (table_hbm, table),
             (by_date, passed))
        )
    ]
    has_up = a > 0
    has_down = a < az_size - 1
    exists = {-1: has_up, 0: None, 1: has_down}
    wraps = {t: d + t >= date_size for t in range(date_size)}

    def guarded(step, body):
        if exists[step] is None:
            body()
        else:
            pl.when(exists[step])(body)

    def place_at(az_step, date_step):
        return {"az": a + az_step, "date": lax.rem(d + date_step, date_size), "rg": g}

    other_core = {"az": a, "date": d, "rg": 1 - g}
    peers = [(o, t) for o in (-1, 0, 1) for t in range(date_size) if (o, t) != (0, 0)]

    barrier = pltpu.get_barrier_semaphore()
    pl.semaphore_signal(barrier, inc=1, device_id=other_core, device_id_type=MESH)
    for o, t in peers:
        if o >= 0:
            @pl.when(jnp.logical_and(jnp.logical_not(wraps[t]), has_down if o else True))
            def _(o=o, t=t):
                pl.semaphore_signal(barrier, inc=1, device_id=place_at(o, t), device_id_type=MESH)
    for load in loads[:3]:
        load.start()

    @pl.when(jnp.logical_not(has_up))
    def _():
        margin[0] = jnp.zeros(margin.shape[1:], margin.dtype)
        far[:, :, 0:REACH] = jnp.zeros((date_size - 1, 2, REACH, samples), far.dtype)
        all_kernels[:, 0] = jnp.zeros((date_size,) + all_kernels.shape[2:], jnp.float32)

    @pl.when(jnp.logical_not(has_down))
    def _():
        margin[1] = jnp.zeros(margin.shape[1:], margin.dtype)
        far[:, :, REACH + lines :] = jnp.zeros((date_size - 1, 2, REACH, samples), far.dtype)
        all_kernels[:, 2] = jnp.zeros((date_size,) + all_kernels.shape[2:], jnp.float32)

    no_side = jnp.zeros((date_size, HALF, ifg.shape[2]), ifg.dtype)

    @pl.when(g == 0)
    def _():
        ifg[:, 0:HALF] = no_side

    @pl.when(g != 0)
    def _():
        ifg[:, HALF + samples :] = no_side

    taken = {
        1: (lines - REACH, REACH, 0), 0: (0, lines, REACH), -1: (0, REACH, REACH + lines),
    }

    def send(o, t, kind, target):
        slot = (date_size - t) % date_size
        spot = PLACE[o]
        first, size, land = taken[o]
        if kind == 0 and t == 0:
            src = image_hbm.at[:, 0, pl.ds(first, size), :]
            dst = margin.at[0 if o == 1 else 1]
        elif kind == 0:
            src = tile.at[:, pl.ds(first, size), :]
            dst = far.at[slot - 1, :, pl.ds(land, size), :]
        else:
            src, dst = kernels, all_kernels.at[slot, spot]
        return pltpu.make_async_remote_copy(
            src_ref=src, dst_ref=dst,
            send_sem=send_sem.at[t, spot, kind],
            recv_sem=recv_sem.at[slot, spot, kind],
            device_id=target, device_id_type=MESH,
        )

    def push(o, t, kind):
        send(o, t, kind, place_at(o, t)).start()

    pl.semaphore_wait(barrier, has_up.astype(jnp.int32) * (d + 1) + d + 1)
    for o, t in peers:
        if o <= 0:
            @pl.when(jnp.logical_and(wraps[t] if t else True, has_up if o else True))
            def _(o=o, t=t):
                pl.semaphore_signal(
                    ready.at[PLACE[-o], (date_size - t) % date_size], inc=1,
                    device_id=place_at(o, t), device_id_type=MESH)

    leads = jnp.logical_or(d == 0, g == 1)

    @pl.when(jnp.logical_and(has_up, leads))
    def _():
        push(-1, 0, 0)

    for load in loads[:2]:
        load.wait()
    shifts = jnp.broadcast_to(offsets[0:1, :].astype(jnp.float32), (TAPS, lines))
    held = jnp.concatenate([taps[:, 0], shifts], axis=1)
    kernels[...] = held
    all_kernels[0, 1] = held

    @pl.when(jnp.logical_and(has_up, leads))
    def _():
        push(-1, 0, 1)

    loads[2].wait()
    for c in range(2):
        tile[c] = image[c, 0].astype(jnp.bfloat16)
    for t in range(1, date_size):
        @pl.when(wraps[t])
        def _(t=t):
            @pl.when(has_up)
            def _():
                push(-1, t, 1)
                push(-1, t, 0)

            push(0, t, 1)
            push(0, t, 0)

    @pl.when(jnp.logical_and(has_up, jnp.logical_not(leads)))
    def _():
        push(-1, 0, 1)
        push(-1, 0, 0)

    for load in loads[3:]:
        load.start()
    for c in range(2):
        value = image[c, 0]
        high = value.astype(jnp.bfloat16)
        near[0, c, REACH : REACH + lines] = high
        near[1, c, REACH : REACH + lines] = (value - high.astype(jnp.float32)).astype(jnp.bfloat16)

    for t in range(1, date_size):
        @pl.when(jnp.logical_not(wraps[t]))
        def _(t=t):
            pl.semaphore_wait(ready.at[PLACE[0], t], 1)
            push(0, t, 1)
            push(0, t, 0)

            @pl.when(has_up)
            def _():
                push(-1, t, 1)
                push(-1, t, 0)

    @pl.when(has_down)
    def _():
        pl.semaphore_wait(ready.at[PLACE[1], 0], 1)
        for t in range(1, date_size):
            @pl.when(wraps[t])
            def _(t=t):
                push(1, t, 1)
                push(1, t, 0)

        push(1, 0, 1)
        push(1, 0, 0)
        for t in range(1, date_size):
            @pl.when(jnp.logical_not(wraps[t]))
            def _(t=t):
                pl.semaphore_wait(ready.at[PLACE[1], t], 1)
                push(1, t, 1)
                push(1, t, 0)

    def arrived(slot):
        t = (date_size - slot) % date_size
        for o in (-1, 0, 1):
            if (o, t) != (0, 0):
                def _(o=o):
                    for kind in (1, 0):
                        send(o, t, kind, place_at(-o, slot)).wait_recv()
                guarded(-o, _)

    def side(slot):
        return pltpu.make_async_remote_copy(
            src_ref=ifg.at[slot, pl.ds(pl.multiple_of(samples - (samples - HALF) * g, HALF), HALF)],
            dst_ref=ifg.at[slot, pl.ds(pl.multiple_of((samples + HALF) * g, HALF), HALF)],
            send_sem=side_sem.at[0, slot], recv_sem=side_sem.at[1, slot],
            device_id=other_core, device_id_type=MESH,
        )

    def side_arrived(slot):
        pltpu.make_async_remote_copy(
            src_ref=ifg.at[slot, pl.ds(pl.multiple_of(samples - (samples - HALF) * g, HALF), HALF)],
            dst_ref=ifg.at[slot, pl.ds(pl.multiple_of((samples + HALF) * (1 - g), HALF), HALF)],
            send_sem=side_sem.at[0, slot], recv_sem=side_sem.at[1, slot],
            device_id=other_core, device_id_type=MESH,
        ).wait_recv()

    span = lines + 2 * REACH
    wide_lines = 4 * HALF
    source = lax.broadcasted_iota(jnp.int32, (span, wide_lines), 0)
    place = lax.broadcasted_iota(jnp.int32, (span, wide_lines), 1)
    distance = (source - place - (RIM - (TAPS // 2 - 1))).astype(jnp.float32)

    def resample(slot):
        above, own_rows, below = (all_kernels[slot, i] for i in range(3))
        weights = jnp.concatenate(
            [above[:, HALF:lines], own_rows[:, :lines], below[:, :HALF]], axis=1
        )
        shift = jnp.concatenate(
            [above[:, lines + HALF :], own_rows[:, lines:], below[:, lines : lines + HALF]], axis=1
        )
        gap = distance - shift[0:1]
        band = jnp.zeros((span, wide_lines), jnp.float32)
        for k in range(TAPS):
            band = jnp.where(gap == float(k), weights[k : k + 1], band)
        band_high = band.astype(jnp.bfloat16)
        band_low = (band - band_high.astype(jnp.float32)).astype(jnp.bfloat16)
        band_both = jnp.concatenate([band_high, band_low], axis=1)
        total = None
        for i in range(1 if slot else 2):
            columns = [far[slot - 1, c] if slot else near[i, c] for c in range(2)]
            product = lax.dot_general(
                jnp.concatenate(columns, axis=1), band_both, (((0,), (0,)), ((), ())),
                preferred_element_type=jnp.float32,
            )
            product = product[:, :wide_lines] + product[:, wide_lines:]
            total = product if total is None else total + product
        total = total.astype(jnp.bfloat16).astype(jnp.float32)
        return total[:samples], total[samples:]

    def combine(slot):
        if slot == 0:
            for i in range(2):
                for c in range(2):
                    value = margin[i, c]
                    high = value.astype(jnp.bfloat16)
                    at = slice(0, REACH) if i == 0 else slice(REACH + lines, span)
                    near[0, c, at] = high
                    near[1, c, at] = (value - high.astype(jnp.float32)).astype(jnp.bfloat16)
        real, imag = resample(slot)
        if slot == 0:
            own[0], own[1] = real, imag
            real_part, imag_part = real * real + imag * imag, jnp.zeros_like(real)
        else:
            real_part = own[0] * real + own[1] * imag
            imag_part = own[1] * real - own[0] * imag
        ifg[slot, HALF : HALF + samples, :wide_lines] = real_part.astype(jnp.bfloat16)
        ifg[slot, HALF : HALF + samples, wide_lines:] = imag_part.astype(jnp.bfloat16)
        side(slot).start()

    arrived(0)
    combine(0)
    for j in range(1, date_size):
        arrived(j)
        combine(j)
    for load in loads[3:]:
        load.wait()
    side_arrived(0)
    if alone is not None:
        alone[...] = filter_patches(ifg.at[0], table, spec, power_sum, shaped, back, True)
    for j in range(1, date_size):
        side_arrived(j)

    for o, t in peers:
        def _(o=o, t=t):
            for kind in (1, 0):
                send(o, t, kind, place_at(o, t)).wait_send()
        guarded(o, _)
    for slot in range(date_size):
        side(slot).wait_send()


def filter_kernel(date_size, ifg, table, by_date, *rest):
    alone = None
    if date_size == 2:
        alone, *rest = rest
    out, results, blank, partner, spec, power_sum, shaped, back, sem, read_sem = rest
    matches = out.shape[0]
    d = lax.axis_index("date")
    read = pltpu.make_async_copy(by_date, partner, read_sem)
    read.start()

    def deliver(m, c, source):
        return pltpu.make_async_copy(source, out.at[m, c, 0], sem.at[m, c])

    if alone is not None:
        blank[...] = jnp.zeros(blank.shape, blank.dtype)
        results[0] = filter_patches(ifg.at[1], table, spec, power_sum, shaped, back, False)
        read.wait()
        for m in range(matches):
            @pl.when(partner[d, m] == d)
            def _(m=m):
                deliver(m, 0, alone).start()
                deliver(m, 1, blank).start()

            @pl.when(partner[d, m] != d)
            def _(m=m):
                for c in range(2):
                    deliver(m, c, results.at[0, pl.ds(c * PATCH, PATCH)]).start()
    else:
        read.wait()
        for m in range(matches):
            slot = lax.rem(partner[d, m] - d + date_size, date_size)
            results[m] = filter_patches(
                ifg.at[slot], table, spec, power_sum, shaped, back, False)
            for c in range(2):
                deliver(m, c, results.at[m, pl.ds(c * PATCH, PATCH)]).start()
    for m in range(matches):
        for c in range(2):
            deliver(m, c, results.at[0, pl.ds(c * PATCH, PATCH)]).wait()


def per_device(az_size, date_size, image_stack, tap_weights, offsets, matchings):
    lines, samples = image_stack.shape[2:]
    assert image_stack.shape[1] == 1 and lines == PATCH
    matches = matchings.shape[0]
    hbm = pl.BlockSpec(memory_space=pltpu.HBM)
    vmem = pl.BlockSpec(memory_space=pltpu.VMEM)
    constants = tables()
    alone = date_size == 2
    passed = [
        pltpu.VMEM((date_size, samples + 2 * HALF, 8 * HALF), jnp.bfloat16),
        pltpu.VMEM(constants.shape, jnp.bfloat16),
        pltpu.VMEM((date_size, matches), jnp.int32),
    ]
    if alone:
        passed.append(pltpu.VMEM((lines, samples), jnp.float32))
    passed = pl.pallas_call(
        functools.partial(stack_kernel, az_size, date_size),
        out_shape=passed,
        in_specs=[hbm] * 5,
        out_specs=[vmem] * len(passed),
        scratch_shapes=(scratch_of_filter(samples, HALF_LANES) if alone else []) + [
            pltpu.VMEM(image_stack.shape, jnp.float32),
            pltpu.VMEM(tap_weights.shape, jnp.float32),
            pltpu.VMEM(offsets.shape, jnp.int32),
            pltpu.VMEM((2, lines, samples), jnp.bfloat16),
            pltpu.VMEM((TAPS, 2 * lines), jnp.float32),
            pltpu.VMEM((2, 2, lines + 2 * REACH, samples), jnp.bfloat16),
            pltpu.VMEM((date_size - 1, 2, lines + 2 * REACH, samples), jnp.bfloat16),
            pltpu.VMEM((2, 2, REACH, samples), jnp.float32),
            pltpu.VMEM((date_size, 3, TAPS, 2 * lines), jnp.float32),
            pltpu.VMEM((2, samples, 4 * HALF), jnp.float32),
            pltpu.SemaphoreType.DMA((5,)),
            pltpu.SemaphoreType.DMA((date_size, 3, 2)),
            pltpu.SemaphoreType.DMA((date_size, 3, 2)),
            pltpu.SemaphoreType.DMA((2, date_size)),
            pltpu.SemaphoreType.REGULAR((3, date_size)),
        ],
        compiler_params=pltpu.CompilerParams(collective_id=0, has_side_effects=True),
    )(image_stack, tap_weights, offsets, jnp.asarray(constants), matchings.T)
    return pl.pallas_call(
        functools.partial(filter_kernel, date_size),
        out_shape=jax.ShapeDtypeStruct((matches, 2, 1, lines, samples), jnp.float32),
        in_specs=[vmem] * len(passed),
        out_specs=hbm,
        scratch_shapes=[
            pltpu.VMEM((1 if alone else matches, 2 * lines, samples), jnp.float32),
            pltpu.VMEM((lines, samples), jnp.float32),
            pltpu.SMEM((date_size, matches), jnp.int32),
        ] + scratch_of_filter(samples, LANES) + [
            pltpu.SemaphoreType.DMA((matches, 2)),
            pltpu.SemaphoreType.DMA,
        ],
        compiler_params=pltpu.CompilerParams(vmem_limit_bytes=24 << 20),
    )(*passed)


def solution(mesh):
    placed = (
        P(None, ("parts", "date"), "az", "rg"),
        P(None, ("parts", "date"), "az"),
        P(("parts", "date"), "az"),
        P(),
    )
    assert mesh.shape["rg"] == 2
    return jax.shard_map(
        functools.partial(per_device, mesh.shape["az"], mesh.shape["date"]),
        mesh=mesh,
        in_specs=placed,
        out_specs=P(None, None, ("parts", "date"), "az", "rg"),
        check_vma=False,
    )
```

```python
import functools
import math

import jax
import jax.numpy as jnp
import ml_dtypes
import numpy as np
from jax import lax
from jax.experimental import pallas as pl
from jax.experimental.pallas import tpu as pltpu
from jax.sharding import PartitionSpec as P

TAPS = 8
SHIFT_MAX = 12
PATCH = 64
HALF = PATCH // 2
RIM = SHIFT_MAX + TAPS // 2
REACH = RIM + HALF
GROUPS = 4
LANES = GROUPS * PATCH
HALF_LANES = 128
HALF_GROUP = HALF + 3
MESH = pl.DeviceIdType.MESH
BF16 = ml_dtypes.bfloat16
PLACE = {1: 0, 0: 1, -1: 2}


def fourier_table(sine_sign, table_scale):
    ids = np.arange(PATCH)
    angles = ((ids[:, None] * ids[None, :]) % PATCH) * (2.0 * math.pi / PATCH)
    cosine = np.cos(angles) * table_scale
    sine = np.sin(angles) * (sine_sign * table_scale)
    table = np.block([[cosine, -sine], [sine, cosine]]).astype(np.float32)
    return table.astype(BF16).astype(np.float32)


def tables():
    forward = fourier_table(1.0, 1.0)
    inverse = fourier_table(-1.0, 1.0 / PATCH)
    window = np.sin(math.pi * (np.arange(PATCH, dtype=np.float32) + 0.5) / PATCH) ** 2
    wide = 2 * PATCH
    line_in = np.zeros((2, wide, 2, GROUPS, PATCH), np.float32)
    line_out = np.zeros((2, PATCH, 2, GROUPS, PATCH), np.float32)
    real_in = np.zeros((wide, 2, HALF_LANES), np.float32)
    real_out = np.zeros((PATCH, 2, HALF_LANES), np.float32)
    real_ring = np.zeros((HALF_LANES, HALF_LANES), np.float32)
    split_f = forward.reshape(2, PATCH, 2, PATCH)
    split_i = inverse.reshape(2, PATCH, 2, PATCH)
    for r in range(3):
        line_in[:, r * HALF : r * HALF + PATCH, :, r] = split_f
        for at in range(HALF_GROUP):
            f, lane = (at - 1) % PATCH, r * HALF_GROUP + at
            real_in[r * HALF : r * HALF + PATCH, :, lane] = split_f[0, :, :, f]
            if 0 < at < HALF_GROUP - 1:
                real_ring[lane - 1 : lane + 2, lane] = 1.0
        for line in range(PATCH):
            u = line + HALF - HALF * r
            if 0 <= u < PATCH:
                line_out[:, line, :, r] = split_i[:, :, :, u].transpose(2, 0, 1) * window[u]
                for at in range(1, HALF_GROUP - 1):
                    f = at - 1
                    times = 1.0 if f in (0, HALF) else 2.0
                    real_out[line, :, r * HALF_GROUP + at] = split_i[:, f, 0, u] * window[u] * times
    line_in = line_in.reshape(2 * wide, 2 * LANES).astype(BF16)
    line_out = line_out.reshape(wide, 2 * LANES)
    high = line_out.astype(BF16)
    low = (line_out - high.astype(np.float32)).astype(BF16)
    ids = np.arange(LANES)
    gap = (ids[:, None] - ids[None, :]) % PATCH
    same = ids[:, None] // PATCH == ids[None, :] // PATCH
    ring = (((gap <= 1) | (gap == PATCH - 1)) & same).astype(BF16)
    turns = np.concatenate([forward.T, inverse.T], axis=0).astype(BF16)
    rows = np.broadcast_to(np.tile(window, 2)[:, None], (wide, wide)).astype(np.float32)
    rows_high = rows.astype(BF16)
    rows_low = (rows - rows_high.astype(np.float32)).astype(BF16)
    last = np.concatenate([ring, turns, np.concatenate([rows_high, rows_low], axis=0)], axis=1)
    real_in = real_in.reshape(wide, 2 * HALF_LANES).astype(BF16)
    real_out = real_out.reshape(PATCH, 2 * HALF_LANES)
    real_high = real_out.astype(BF16)
    real_low = (real_out - real_high.astype(np.float32)).astype(BF16)
    real = np.concatenate([real_in, np.concatenate([real_high, real_low], axis=0)], axis=1)
    rest = np.zeros((wide, 2 * LANES), BF16)
    rest[:, :HALF_LANES] = real_ring.astype(BF16)
    return np.concatenate([line_in, high, low, last, real, rest], axis=0)


class Filter:
    def __init__(self, ifg, table, real, spectra, back, edge, spec, power_sum, shaped):
        wide = 2 * PATCH
        self.ifg, self.table = ifg, table
        self.spectra, self.back, self.edge = spectra, back, edge
        self.spec, self.power_sum, self.shaped = spec, power_sum, shaped
        self.depth = (1 if real else 2) * wide
        self.lanes = lanes = HALF_LANES if real else LANES
        columns = spec.shape[0]
        self.inner, self.outer = range(1, columns - 1), (0, columns - 1)
        rows = ifg.shape[0]
        self.inside = ((HALF, rows - 2 * HALF),)
        self.outside = ((0, HALF), (rows - HALF, HALF))
        self.line_in = table[6 * wide : 7 * wide, 0:LANES] if real else table[0 : 2 * wide]
        self.ring = table[7 * wide :, 0:lanes] if real else table[4 * wide : 6 * wide, 0:LANES]
        self.line_out = table[6 * wide : 7 * wide, LANES:] if real else table[2 * wide : 4 * wide]
        self.forward = table[4 * wide : 5 * wide, LANES : LANES + wide]
        self.inverse = table[5 * wide : 6 * wide, LANES : LANES + wide]

    def lines(self, pieces):
        rows = [self.ifg[first : first + size, : self.depth] for first, size in pieces]
        rows = rows[0] if len(rows) == 1 else jnp.concatenate(rows, axis=0)
        made = jnp.dot(rows, self.line_in, preferred_element_type=jnp.float32)
        made, at = made.astype(jnp.bfloat16), 0
        for first, size in pieces:
            self.spectra[first : first + size] = made[at : at + size]
            at += size

    def samples(self, which):
        for q in which:
            rows = self.spectra[q * HALF : q * HALF + PATCH]
            block = jnp.concatenate([rows[:, : self.lanes], rows[:, self.lanes :]], axis=0)
            spectrum = jnp.dot(self.forward, block, preferred_element_type=jnp.float32)
            self.spec[q] = spectrum
            re, im = spectrum[:PATCH], spectrum[PATCH:]
            power = re * re + im * im
            summed = power + pltpu.roll(power, 1, 0) + pltpu.roll(power, PATCH - 1, 0)
            self.power_sum[q * PATCH : (q + 1) * PATCH] = summed.astype(jnp.bfloat16)

    def gain(self, which):
        if len(which) == 2:
            power = jnp.concatenate(
                [self.power_sum[q * PATCH : (q + 1) * PATCH] for q in which], axis=0)
        else:
            power = self.power_sum[which[0] * PATCH : (which[-1] + 1) * PATCH]
        smooth = jnp.dot(power, self.ring, preferred_element_type=jnp.float32)
        gains = lax.rsqrt(lax.rsqrt(1.0 + smooth * (1.0 / (9.0 * PATCH * PATCH))))
        for i, q in enumerate(which):
            gain = gains[i * PATCH : (i + 1) * PATCH]
            self.shaped[q, :PATCH] = (self.spec[q, :PATCH] * gain).astype(jnp.bfloat16)
            self.shaped[q, PATCH:] = (self.spec[q, PATCH:] * gain).astype(jnp.bfloat16)

    def ranged(self, which):
        wide = 2 * PATCH
        pieces = [
            self.table[i * wide : (i + 1) * wide, LANES + wide : LANES + 2 * wide].astype(
                jnp.float32)
            for i in (4, 5)
        ]
        weights = jnp.concatenate([pieces[0] + pieces[1]] * (self.lanes // wide), axis=1)
        for q in which:
            value = jnp.dot(
                self.inverse, self.shaped[q], preferred_element_type=jnp.float32) * weights
            yield q, [[value[c * PATCH + i * HALF : c * PATCH + (i + 1) * HALF]
                       for c in range(2)] for i in range(2)]

    def join(self, j, second, first):
        for c in range(2):
            self.back[j * HALF : (j + 1) * HALF, c * self.lanes : (c + 1) * self.lanes] = (
                (second[c] + first[c]).astype(jnp.bfloat16))

    def samples_back_inner(self):
        held = None
        for q, halves in self.ranged(self.inner):
            if held is None:
                self.edge[0, 0], self.edge[0, 1] = halves[0]
            else:
                self.join(q - 1, held, halves[0])
            held = halves[1]
        self.edge[1, 0], self.edge[1, 1] = held

    def samples_back_outer(self):
        (_, left), (last, right) = self.ranged(self.outer)
        self.join(0, left[1], [self.edge[0, 0], self.edge[0, 1]])
        self.join(last - 1, [self.edge[1, 0], self.edge[1, 1]], right[0])

    def lines_back(self):
        split = lax.dot_general(
            self.line_out, self.back[...], (((1,), (1,)), ((), ())),
            preferred_element_type=jnp.float32,
        )
        tall = split.shape[0] // 2
        return split[:tall] + split[tall:]


def run_inner(*filters):
    for one in filters:
        one.lines(one.inside)
    for one in filters:
        one.samples(one.inner)
    for one in filters:
        one.gain(one.inner)
    for one in filters:
        one.samples_back_inner()


def run_outer(*filters):
    for one in filters:
        one.lines(one.outside)
    for one in filters:
        one.samples(one.outer)
    for one in filters:
        one.gain(one.outer)
    for one in filters:
        one.samples_back_outer()
    return [one.lines_back() for one in filters]


def kept_of_filter(samples, lanes):
    return [
        pltpu.VMEM((samples + 2 * HALF, 2 * lanes), jnp.bfloat16),
        pltpu.VMEM((samples, 2 * lanes), jnp.bfloat16),
        pltpu.VMEM((2, 2, HALF, lanes), jnp.float32),
    ]


def scratch_of_filter(samples, lanes):
    columns = samples // HALF + 1
    return [
        pltpu.VMEM((columns, 2 * PATCH, lanes), jnp.float32),
        pltpu.VMEM((columns * PATCH, lanes), jnp.bfloat16),
        pltpu.VMEM((columns, 2 * PATCH, lanes), jnp.bfloat16),
    ]


def stack_kernel(
    az_size, date_size, image_hbm, taps_hbm, offsets_hbm, table_hbm, by_date, ifg, table, passed,
    *rest,
):
    if date_size == 2:
        kept, scratch, rest = rest[:6], rest[6:12], rest[12:]
    (
        image, taps, offsets, tile, kernels, near, far, margin, all_kernels, own,
        load_sem, send_sem, recv_sem, side_sem, ready,
    ) = rest
    a = lax.axis_index("az")
    d = lax.axis_index("date")
    g = lax.axis_index("rg")
    lines = image.shape[2]
    samples = image.shape[3]
    wide = 2 * PATCH
    loads = [
        pltpu.make_async_copy(source, target, load_sem.at[i])
        for i, (source, target) in enumerate(
            ((offsets_hbm, offsets), (taps_hbm, taps), (image_hbm, image), (table_hbm, table),
             (by_date, passed))
        )
    ]
    has_up = a > 0
    has_down = a < az_size - 1
    exists = {-1: has_up, 0: None, 1: has_down}
    wraps = {t: d + t >= date_size for t in range(date_size)}

    def guarded(step, body):
        if exists[step] is None:
            body()
        else:
            pl.when(exists[step])(body)

    def place_at(az_step, date_step):
        return {"az": a + az_step, "date": lax.rem(d + date_step, date_size), "rg": g}

    other_core = {"az": a, "date": d, "rg": 1 - g}
    peers = [(o, t) for o in (-1, 0, 1) for t in range(date_size) if (o, t) != (0, 0)]

    barrier = pltpu.get_barrier_semaphore()
    pl.semaphore_signal(barrier, inc=1, device_id=other_core, device_id_type=MESH)
    for o, t in peers:
        if o >= 0:
            @pl.when(jnp.logical_and(jnp.logical_not(wraps[t]), has_down if o else True))
            def _(o=o, t=t):
                pl.semaphore_signal(barrier, inc=1, device_id=place_at(o, t), device_id_type=MESH)
    for load in loads[:3]:
        load.start()

    @pl.when(jnp.logical_not(has_up))
    def _():
        margin[0] = jnp.zeros(margin.shape[1:], margin.dtype)
        far[:, :, 0:REACH] = jnp.zeros((date_size - 1, 2, REACH, samples), far.dtype)
        all_kernels[:, 0] = jnp.zeros((date_size,) + all_kernels.shape[2:], jnp.float32)

    @pl.when(jnp.logical_not(has_down))
    def _():
        margin[1] = jnp.zeros(margin.shape[1:], margin.dtype)
        far[:, :, REACH + lines :] = jnp.zeros((date_size - 1, 2, REACH, samples), far.dtype)
        all_kernels[:, 2] = jnp.zeros((date_size,) + all_kernels.shape[2:], jnp.float32)

    no_side = jnp.zeros((date_size, HALF, ifg.shape[2]), ifg.dtype)

    @pl.when(g == 0)
    def _():
        ifg[:, 0:HALF] = no_side

    @pl.when(g != 0)
    def _():
        ifg[:, HALF + samples :] = no_side

    taken = {
        1: (lines - REACH, REACH, 0), 0: (0, lines, REACH), -1: (0, REACH, REACH + lines),
    }

    def send(o, t, kind, target):
        slot = (date_size - t) % date_size
        spot = PLACE[o]
        first, size, land = taken[o]
        if kind == 0 and t == 0:
            src = image_hbm.at[:, 0, pl.ds(first, size), :]
            dst = margin.at[0 if o == 1 else 1]
        elif kind == 0:
            src = tile.at[:, pl.ds(first, size), :]
            dst = far.at[slot - 1, :, pl.ds(land, size), :]
        else:
            src, dst = kernels, all_kernels.at[slot, spot]
        return pltpu.make_async_remote_copy(
            src_ref=src, dst_ref=dst,
            send_sem=send_sem.at[t, spot, kind],
            recv_sem=recv_sem.at[slot, spot, kind],
            device_id=target, device_id_type=MESH,
        )

    def push(o, t, kind):
        send(o, t, kind, place_at(o, t)).start()

    pl.semaphore_wait(barrier, has_up.astype(jnp.int32) * (d + 1) + d + 1)
    for o, t in peers:
        if o <= 0:
            @pl.when(jnp.logical_and(wraps[t] if t else True, has_up if o else True))
            def _(o=o, t=t):
                pl.semaphore_signal(
                    ready.at[PLACE[-o], (date_size - t) % date_size], inc=1,
                    device_id=place_at(o, t), device_id_type=MESH)

    leads = jnp.logical_or(d == 0, g == 1)

    @pl.when(jnp.logical_and(has_up, leads))
    def _():
        push(-1, 0, 0)

    for load in loads[:2]:
        load.wait()
    shifts = jnp.broadcast_to(offsets[0:1, :].astype(jnp.float32), (TAPS, lines))
    held = jnp.concatenate([taps[:, 0], shifts], axis=1)
    kernels[...] = held
    all_kernels[0, 1] = held

    @pl.when(jnp.logical_and(has_up, leads))
    def _():
        push(-1, 0, 1)

    loads[2].wait()
    for c in range(2):
        tile[c] = image[c, 0].astype(jnp.bfloat16)
    for t in range(1, date_size):
        @pl.when(wraps[t])
        def _(t=t):
            @pl.when(has_up)
            def _():
                push(-1, t, 1)
                push(-1, t, 0)

            push(0, t, 1)
            push(0, t, 0)

    @pl.when(jnp.logical_and(has_up, jnp.logical_not(leads)))
    def _():
        push(-1, 0, 1)
        push(-1, 0, 0)

    for load in loads[3:]:
        load.start()
    for c in range(2):
        value = image[c, 0]
        high = value.astype(jnp.bfloat16)
        near[0, c, REACH : REACH + lines] = high
        near[1, c, REACH : REACH + lines] = (value - high.astype(jnp.float32)).astype(jnp.bfloat16)

    for t in range(1, date_size):
        @pl.when(jnp.logical_not(wraps[t]))
        def _(t=t):
            pl.semaphore_wait(ready.at[PLACE[0], t], 1)
            push(0, t, 1)
            push(0, t, 0)

            @pl.when(has_up)
            def _():
                push(-1, t, 1)
                push(-1, t, 0)

    @pl.when(has_down)
    def _():
        pl.semaphore_wait(ready.at[PLACE[1], 0], 1)
        for t in range(1, date_size):
            @pl.when(wraps[t])
            def _(t=t):
                push(1, t, 1)
                push(1, t, 0)

        push(1, 0, 1)
        push(1, 0, 0)
        for t in range(1, date_size):
            @pl.when(jnp.logical_not(wraps[t]))
            def _(t=t):
                pl.semaphore_wait(ready.at[PLACE[1], t], 1)
                push(1, t, 1)
                push(1, t, 0)

    def arrived(slot):
        t = (date_size - slot) % date_size
        for o in (-1, 0, 1):
            if (o, t) != (0, 0):
                def _(o=o):
                    for kind in (1, 0):
                        send(o, t, kind, place_at(-o, slot)).wait_recv()
                guarded(-o, _)

    def side(slot):
        return pltpu.make_async_remote_copy(
            src_ref=ifg.at[slot, pl.ds(pl.multiple_of(samples - (samples - HALF) * g, HALF), HALF)],
            dst_ref=ifg.at[slot, pl.ds(pl.multiple_of((samples + HALF) * g, HALF), HALF)],
            send_sem=side_sem.at[0, slot], recv_sem=side_sem.at[1, slot],
            device_id=other_core, device_id_type=MESH,
        )

    def side_arrived(slot):
        pltpu.make_async_remote_copy(
            src_ref=ifg.at[slot, pl.ds(pl.multiple_of(samples - (samples - HALF) * g, HALF), HALF)],
            dst_ref=ifg.at[slot, pl.ds(pl.multiple_of((samples + HALF) * (1 - g), HALF), HALF)],
            send_sem=side_sem.at[0, slot], recv_sem=side_sem.at[1, slot],
            device_id=other_core, device_id_type=MESH,
        ).wait_recv()

    span = lines + 2 * REACH
    wide_lines = 4 * HALF
    source = lax.broadcasted_iota(jnp.int32, (span, wide_lines), 0)
    place = lax.broadcasted_iota(jnp.int32, (span, wide_lines), 1)
    distance = (source - place - (RIM - (TAPS // 2 - 1))).astype(jnp.float32)

    def resample(slot):
        above, own_rows, below = (all_kernels[slot, i] for i in range(3))
        weights = jnp.concatenate(
            [above[:, HALF:lines], own_rows[:, :lines], below[:, :HALF]], axis=1
        )
        shift = jnp.concatenate(
            [above[:, lines + HALF :], own_rows[:, lines:], below[:, lines : lines + HALF]], axis=1
        )
        gap = distance - shift[0:1]
        band = jnp.zeros((span, wide_lines), jnp.float32)
        for k in range(TAPS):
            band = jnp.where(gap == float(k), weights[k : k + 1], band)
        band_high = band.astype(jnp.bfloat16)
        band_low = (band - band_high.astype(jnp.float32)).astype(jnp.bfloat16)
        band_both = jnp.concatenate([band_high, band_low], axis=1)
        total = None
        for i in range(1 if slot else 2):
            columns = [far[slot - 1, c] if slot else near[i, c] for c in range(2)]
            product = lax.dot_general(
                jnp.concatenate(columns, axis=1), band_both, (((0,), (0,)), ((), ())),
                preferred_element_type=jnp.float32,
            )
            product = product[:, :wide_lines] + product[:, wide_lines:]
            total = product if total is None else total + product
        total = total.astype(jnp.bfloat16).astype(jnp.float32)
        return total[:samples], total[samples:]

    def combine(slot):
        if slot == 0:
            for i in range(2):
                for c in range(2):
                    value = margin[i, c]
                    high = value.astype(jnp.bfloat16)
                    at = slice(0, REACH) if i == 0 else slice(REACH + lines, span)
                    near[0, c, at] = high
                    near[1, c, at] = (value - high.astype(jnp.float32)).astype(jnp.bfloat16)
        real, imag = resample(slot)
        if slot == 0:
            own[0], own[1] = real, imag
            real_part, imag_part = real * real + imag * imag, jnp.zeros_like(real)
        else:
            real_part = own[0] * real + own[1] * imag
            imag_part = own[1] * real - own[0] * imag
        ifg[slot, HALF : HALF + samples, :wide_lines] = real_part.astype(jnp.bfloat16)
        ifg[slot, HALF : HALF + samples, wide_lines:] = imag_part.astype(jnp.bfloat16)
        side(slot).start()

    arrived(0)
    combine(0)
    for j in range(1, date_size):
        arrived(j)
        combine(j)
    for load in loads[3:]:
        load.wait()
    if date_size == 2:
        run_inner(
            Filter(ifg.at[1], table, False, *kept[:3], *scratch[:3]),
            Filter(ifg.at[0], table, True, *kept[3:], *scratch[3:]),
        )
    for j in range(date_size):
        side_arrived(j)

    for o, t in peers:
        def _(o=o, t=t):
            for kind in (1, 0):
                send(o, t, kind, place_at(o, t)).wait_send()
        guarded(o, _)
    for slot in range(date_size):
        side(slot).wait_send()


def filter_kernel(date_size, ifg, table, by_date, *rest):
    alone = date_size == 2
    kept, rest = (rest[:6], rest[6:]) if alone else ([], rest)
    out, results, partner, sem, read_sem, *rest = rest
    kept, scratch = (kept, rest) if alone else (rest[:3], rest[3:])
    matches = out.shape[0]
    d = lax.axis_index("date")
    read = pltpu.make_async_copy(by_date, partner, read_sem)
    read.start()

    def deliver(m, c, spot):
        return pltpu.make_async_copy(
            results.at[spot, pl.ds(c * PATCH, PATCH)], out.at[m, c, 0], sem.at[m, c])

    if alone:
        results[0, PATCH:] = jnp.zeros((PATCH, results.shape[2]), results.dtype)
        results[1], results[0, :PATCH] = run_outer(
            Filter(ifg.at[1], table, False, *kept[:3], *scratch[:3]),
            Filter(ifg.at[0], table, True, *kept[3:], *scratch[3:]),
        )
        read.wait()
        for m in range(matches):
            spot = lax.rem(partner[d, m] - d + date_size, date_size)
            for c in range(2):
                deliver(m, c, spot).start()
    else:
        read.wait()
        for m in range(matches):
            spot = lax.rem(partner[d, m] - d + date_size, date_size)
            one = Filter(ifg.at[spot], table, False, *kept, *scratch)
            run_inner(one)
            results[m] = run_outer(one)[0]
            for c in range(2):
                deliver(m, c, m).start()
    for m in range(matches):
        for c in range(2):
            deliver(m, c, 0).wait()


def per_device(az_size, date_size, image_stack, tap_weights, offsets, matchings):
    lines, samples = image_stack.shape[2:]
    assert image_stack.shape[1] == 1 and lines == PATCH
    matches = matchings.shape[0]
    hbm = pl.BlockSpec(memory_space=pltpu.HBM)
    vmem = pl.BlockSpec(memory_space=pltpu.VMEM)
    constants = tables()
    alone = date_size == 2
    passed = [
        pltpu.VMEM((date_size, samples + 2 * HALF, 8 * HALF), jnp.bfloat16),
        pltpu.VMEM(constants.shape, jnp.bfloat16),
        pltpu.VMEM((date_size, matches), jnp.int32),
    ]
    if alone:
        passed += kept_of_filter(samples, LANES) + kept_of_filter(samples, HALF_LANES)
    scratch = scratch_of_filter(samples, LANES)
    if alone:
        scratch += scratch_of_filter(samples, HALF_LANES)
    else:
        scratch = kept_of_filter(samples, LANES) + scratch
    passed = pl.pallas_call(
        functools.partial(stack_kernel, az_size, date_size),
        out_shape=passed,
        in_specs=[hbm] * 5,
        out_specs=[vmem] * len(passed),
        scratch_shapes=(scratch if alone else []) + [
            pltpu.VMEM(image_stack.shape, jnp.float32),
            pltpu.VMEM(tap_weights.shape, jnp.float32),
            pltpu.VMEM(offsets.shape, jnp.int32),
            pltpu.VMEM((2, lines, samples), jnp.bfloat16),
            pltpu.VMEM((TAPS, 2 * lines), jnp.float32),
            pltpu.VMEM((2, 2, lines + 2 * REACH, samples), jnp.bfloat16),
            pltpu.VMEM((date_size - 1, 2, lines + 2 * REACH, samples), jnp.bfloat16),
            pltpu.VMEM((2, 2, REACH, samples), jnp.float32),
            pltpu.VMEM((date_size, 3, TAPS, 2 * lines), jnp.float32),
            pltpu.VMEM((2, samples, 4 * HALF), jnp.float32),
            pltpu.SemaphoreType.DMA((5,)),
            pltpu.SemaphoreType.DMA((date_size, 3, 2)),
            pltpu.SemaphoreType.DMA((date_size, 3, 2)),
            pltpu.SemaphoreType.DMA((2, date_size)),
            pltpu.SemaphoreType.REGULAR((3, date_size)),
        ],
        compiler_params=pltpu.CompilerParams(collective_id=0, has_side_effects=True),
    )(image_stack, tap_weights, offsets, jnp.asarray(constants), matchings.T)
    return pl.pallas_call(
        functools.partial(filter_kernel, date_size),
        out_shape=jax.ShapeDtypeStruct((matches, 2, 1, lines, samples), jnp.float32),
        in_specs=[vmem] * len(passed),
        out_specs=hbm,
        scratch_shapes=[
            pltpu.VMEM((2 if alone else matches, 2 * lines, samples), jnp.float32),
            pltpu.SMEM((date_size, matches), jnp.int32),
            pltpu.SemaphoreType.DMA((matches, 2)),
            pltpu.SemaphoreType.DMA,
        ] + scratch,
        compiler_params=pltpu.CompilerParams(vmem_limit_bytes=24 << 20),
    )(*passed)


def solution(mesh):
    placed = (
        P(None, ("parts", "date"), "az", "rg"),
        P(None, ("parts", "date"), "az"),
        P(("parts", "date"), "az"),
        P(),
    )
    assert mesh.shape["rg"] == 2
    return jax.shard_map(
        functools.partial(per_device, mesh.shape["az"], mesh.shape["date"]),
        mesh=mesh,
        in_specs=placed,
        out_specs=P(None, None, ("parts", "date"), "az", "rg"),
        check_vma=False,
    )
```

```python
import functools
import math

import jax
import jax.numpy as jnp
import ml_dtypes
import numpy as np
from jax import lax
from jax.experimental import pallas as pl
from jax.experimental.pallas import tpu as pltpu
from jax.sharding import PartitionSpec as P

TAPS = 8
SHIFT_MAX = 12
PATCH = 64
HALF = PATCH // 2
RIM = SHIFT_MAX + TAPS // 2
REACH = RIM + HALF
FINE = 16
GROUPS = 4
LANES = GROUPS * PATCH
HALF_LANES = 128
HALF_GROUP = HALF + 3
MESH = pl.DeviceIdType.MESH
BF16 = ml_dtypes.bfloat16
PLACE = {1: 0, 0: 1, -1: 2}


def fourier_table(sine_sign, table_scale):
    ids = np.arange(PATCH)
    angles = ((ids[:, None] * ids[None, :]) % PATCH) * (2.0 * math.pi / PATCH)
    cosine = np.cos(angles) * table_scale
    sine = np.sin(angles) * (sine_sign * table_scale)
    table = np.block([[cosine, -sine], [sine, cosine]]).astype(np.float32)
    return table.astype(BF16).astype(np.float32)


def tables():
    forward = fourier_table(1.0, 1.0)
    inverse = fourier_table(-1.0, 1.0 / PATCH)
    window = np.sin(math.pi * (np.arange(PATCH, dtype=np.float32) + 0.5) / PATCH) ** 2
    wide = 2 * PATCH
    line_in = np.zeros((2, wide, 2, GROUPS, PATCH), np.float32)
    line_out = np.zeros((2, PATCH, 2, GROUPS, PATCH), np.float32)
    real_in = np.zeros((wide, 2, HALF_LANES), np.float32)
    real_out = np.zeros((PATCH, 2, HALF_LANES), np.float32)
    real_ring = np.zeros((HALF_LANES, HALF_LANES), np.float32)
    split_f = forward.reshape(2, PATCH, 2, PATCH)
    split_i = inverse.reshape(2, PATCH, 2, PATCH)
    for r in range(3):
        line_in[:, r * HALF : r * HALF + PATCH, :, r] = split_f
        for at in range(HALF_GROUP):
            f, lane = (at - 1) % PATCH, r * HALF_GROUP + at
            real_in[r * HALF : r * HALF + PATCH, :, lane] = split_f[0, :, :, f]
            if 0 < at < HALF_GROUP - 1:
                real_ring[lane - 1 : lane + 2, lane] = 1.0
        for line in range(PATCH):
            u = line + HALF - HALF * r
            if 0 <= u < PATCH:
                line_out[:, line, :, r] = split_i[:, :, :, u].transpose(2, 0, 1) * window[u]
                for at in range(1, HALF_GROUP - 1):
                    f = at - 1
                    times = 1.0 if f in (0, HALF) else 2.0
                    real_out[line, :, r * HALF_GROUP + at] = split_i[:, f, 0, u] * window[u] * times
    line_in = line_in.reshape(2 * wide, 2 * LANES).astype(BF16)
    line_out = line_out.reshape(wide, 2 * LANES)
    high = line_out.astype(BF16)
    low = (line_out - high.astype(np.float32)).astype(BF16)
    ids = np.arange(LANES)
    gap = (ids[:, None] - ids[None, :]) % PATCH
    same = ids[:, None] // PATCH == ids[None, :] // PATCH
    ring = (((gap <= 1) | (gap == PATCH - 1)) & same).astype(BF16)
    turns = np.concatenate([forward.T, inverse.T], axis=0).astype(BF16)
    rows = np.broadcast_to(np.tile(window, 2)[:, None], (wide, wide)).astype(np.float32)
    rows_high = rows.astype(BF16)
    rows_low = (rows - rows_high.astype(np.float32)).astype(BF16)
    last = np.concatenate([ring, turns, np.concatenate([rows_high, rows_low], axis=0)], axis=1)
    real_in = real_in.reshape(wide, 2 * HALF_LANES).astype(BF16)
    real_out = real_out.reshape(PATCH, 2 * HALF_LANES)
    real_high = real_out.astype(BF16)
    real_low = (real_out - real_high.astype(np.float32)).astype(BF16)
    real = np.concatenate([real_in, np.concatenate([real_high, real_low], axis=0)], axis=1)
    rest = np.zeros((wide, 2 * LANES), BF16)
    rest[:, :HALF_LANES] = real_ring.astype(BF16)
    return np.concatenate([line_in, high, low, last, real, rest], axis=0)


class Filter:
    def __init__(self, ifg, table, real, spectra, back, edge, spec, power_sum, shaped):
        wide = 2 * PATCH
        self.ifg, self.table = ifg, table
        self.spectra, self.back, self.edge = spectra, back, edge
        self.spec, self.power_sum, self.shaped = spec, power_sum, shaped
        self.depth = (1 if real else 2) * wide
        self.lanes = lanes = HALF_LANES if real else LANES
        columns = spec.shape[0]
        self.inner, self.outer = range(1, columns - 1), (0, columns - 1)
        rows = ifg.shape[0]
        self.inside = ((HALF, rows - 2 * HALF),)
        self.outside = ((0, HALF), (rows - HALF, HALF))
        self.line_in = table[6 * wide : 7 * wide, 0:LANES] if real else table[0 : 2 * wide]
        self.ring = table[7 * wide :, 0:lanes] if real else table[4 * wide : 6 * wide, 0:LANES]
        self.line_out = table[6 * wide : 7 * wide, LANES:] if real else table[2 * wide : 4 * wide]
        self.forward = table[4 * wide : 5 * wide, LANES : LANES + wide]
        self.inverse = table[5 * wide : 6 * wide, LANES : LANES + wide]

    def lines(self, pieces):
        rows = [self.ifg[first : first + size, : self.depth] for first, size in pieces]
        rows = rows[0] if len(rows) == 1 else jnp.concatenate(rows, axis=0)
        made = jnp.dot(rows, self.line_in, preferred_element_type=jnp.float32)
        made, at = made.astype(jnp.bfloat16), 0
        for first, size in pieces:
            self.spectra[first : first + size] = made[at : at + size]
            at += size

    def samples(self, which):
        for q in which:
            rows = self.spectra[q * HALF : q * HALF + PATCH]
            block = jnp.concatenate([rows[:, : self.lanes], rows[:, self.lanes :]], axis=0)
            spectrum = jnp.dot(self.forward, block, preferred_element_type=jnp.float32)
            self.spec[q] = spectrum
            re, im = spectrum[:PATCH], spectrum[PATCH:]
            power = re * re + im * im
            summed = power + pltpu.roll(power, 1, 0) + pltpu.roll(power, PATCH - 1, 0)
            self.power_sum[q * PATCH : (q + 1) * PATCH] = summed.astype(jnp.bfloat16)

    def gain(self, which):
        if len(which) == 2:
            power = jnp.concatenate(
                [self.power_sum[q * PATCH : (q + 1) * PATCH] for q in which], axis=0)
        else:
            power = self.power_sum[which[0] * PATCH : (which[-1] + 1) * PATCH]
        smooth = jnp.dot(power, self.ring, preferred_element_type=jnp.float32)
        gains = lax.rsqrt(lax.rsqrt(1.0 + smooth * (1.0 / (9.0 * PATCH * PATCH))))
        for i, q in enumerate(which):
            gain = gains[i * PATCH : (i + 1) * PATCH]
            self.shaped[q, :PATCH] = (self.spec[q, :PATCH] * gain).astype(jnp.bfloat16)
            self.shaped[q, PATCH:] = (self.spec[q, PATCH:] * gain).astype(jnp.bfloat16)

    def ranged(self, which):
        wide = 2 * PATCH
        pieces = [
            self.table[i * wide : (i + 1) * wide, LANES + wide : LANES + 2 * wide].astype(
                jnp.float32)
            for i in (4, 5)
        ]
        weights = jnp.concatenate([pieces[0] + pieces[1]] * (self.lanes // wide), axis=1)
        for q in which:
            value = jnp.dot(
                self.inverse, self.shaped[q], preferred_element_type=jnp.float32) * weights
            yield q, [[value[c * PATCH + i * HALF : c * PATCH + (i + 1) * HALF]
                       for c in range(2)] for i in range(2)]

    def join(self, j, second, first):
        for c in range(2):
            self.back[j * HALF : (j + 1) * HALF, c * self.lanes : (c + 1) * self.lanes] = (
                (second[c] + first[c]).astype(jnp.bfloat16))

    def samples_back_inner(self):
        held = None
        for q, halves in self.ranged(self.inner):
            if held is None:
                self.edge[0, 0], self.edge[0, 1] = halves[0]
            else:
                self.join(q - 1, held, halves[0])
            held = halves[1]
        self.edge[1, 0], self.edge[1, 1] = held

    def samples_back_outer(self):
        (_, left), (last, right) = self.ranged(self.outer)
        self.join(0, left[1], [self.edge[0, 0], self.edge[0, 1]])
        self.join(last - 1, [self.edge[1, 0], self.edge[1, 1]], right[0])

    def lines_back(self):
        split = lax.dot_general(
            self.line_out, self.back[...], (((1,), (1,)), ((), ())),
            preferred_element_type=jnp.float32,
        )
        tall = split.shape[0] // 2
        return split[:tall] + split[tall:]


def run_inner(*filters):
    for one in filters:
        one.lines(one.inside)
    for one in filters:
        one.samples(one.inner)
    for one in filters:
        one.gain(one.inner)
    for one in filters:
        one.samples_back_inner()


def run_outer(*filters):
    for one in filters:
        one.lines(one.outside)
    for one in filters:
        one.samples(one.outer)
    for one in filters:
        one.gain(one.outer)
    for one in filters:
        one.samples_back_outer()
    return [one.lines_back() for one in filters]


def kept_of_filter(samples, lanes):
    return [
        pltpu.VMEM((samples + 2 * HALF, 2 * lanes), jnp.bfloat16),
        pltpu.VMEM((samples, 2 * lanes), jnp.bfloat16),
        pltpu.VMEM((2, 2, HALF, lanes), jnp.float32),
    ]


def scratch_of_filter(samples, lanes):
    columns = samples // HALF + 1
    return [
        pltpu.VMEM((columns, 2 * PATCH, lanes), jnp.float32),
        pltpu.VMEM((columns * PATCH, lanes), jnp.bfloat16),
        pltpu.VMEM((columns, 2 * PATCH, lanes), jnp.bfloat16),
    ]


def stack_kernel(
    az_size, date_size, image_hbm, taps_hbm, offsets_hbm, table_hbm, by_date, ifg, table, passed,
    *rest,
):
    if date_size == 2:
        kept, scratch, rest = rest[:6], rest[6:12], rest[12:]
    (
        image, taps, offsets, tile, kernels, near, far, margin, all_kernels, bands, own,
        load_sem, send_sem, recv_sem, side_sem, ready,
    ) = rest
    a = lax.axis_index("az")
    d = lax.axis_index("date")
    g = lax.axis_index("rg")
    lines = image.shape[2]
    samples = image.shape[3]
    wide = 2 * PATCH
    loads = [
        pltpu.make_async_copy(source, target, load_sem.at[i])
        for i, (source, target) in enumerate(
            ((offsets_hbm, offsets), (taps_hbm, taps), (image_hbm, image), (table_hbm, table),
             (by_date, passed))
        )
    ]
    has_up = a > 0
    has_down = a < az_size - 1
    exists = {-1: has_up, 0: None, 1: has_down}
    wraps = {t: d + t >= date_size for t in range(date_size)}

    def guarded(step, body):
        if exists[step] is None:
            body()
        else:
            pl.when(exists[step])(body)

    def place_at(az_step, date_step):
        return {"az": a + az_step, "date": lax.rem(d + date_step, date_size), "rg": g}

    other_core = {"az": a, "date": d, "rg": 1 - g}
    peers = [(o, t) for o in (-1, 0, 1) for t in range(date_size) if (o, t) != (0, 0)]

    barrier = pltpu.get_barrier_semaphore()
    pl.semaphore_signal(barrier, inc=1, device_id=other_core, device_id_type=MESH)
    for o, t in peers:
        if o >= 0:
            @pl.when(jnp.logical_and(jnp.logical_not(wraps[t]), has_down if o else True))
            def _(o=o, t=t):
                pl.semaphore_signal(barrier, inc=1, device_id=place_at(o, t), device_id_type=MESH)
    for load in loads[:3]:
        load.start()

    coarse = jnp.zeros((2, REACH - FINE, samples), near.dtype)
    near[1, :, 0 : REACH - FINE] = coarse
    near[1, :, REACH + lines + FINE :] = coarse

    @pl.when(jnp.logical_not(has_up))
    def _():
        near[0, :, 0 : REACH - FINE] = coarse
        margin[0] = jnp.zeros(margin.shape[1:], margin.dtype)
        far[:, :, 0:REACH] = jnp.zeros((date_size - 1, 2, REACH, samples), far.dtype)
        all_kernels[:, 0] = jnp.zeros((date_size,) + all_kernels.shape[2:], jnp.float32)

    @pl.when(jnp.logical_not(has_down))
    def _():
        near[0, :, REACH + lines + FINE :] = coarse
        margin[1] = jnp.zeros(margin.shape[1:], margin.dtype)
        far[:, :, REACH + lines :] = jnp.zeros((date_size - 1, 2, REACH, samples), far.dtype)
        all_kernels[:, 2] = jnp.zeros((date_size,) + all_kernels.shape[2:], jnp.float32)

    no_side = jnp.zeros((date_size, HALF, ifg.shape[2]), ifg.dtype)

    @pl.when(g == 0)
    def _():
        ifg[:, 0:HALF] = no_side

    @pl.when(g != 0)
    def _():
        ifg[:, HALF + samples :] = no_side

    taken = {
        1: (lines - REACH, REACH, 0), 0: (0, lines, REACH), -1: (0, REACH, REACH + lines),
    }

    def send(o, t, kind, target):
        slot = (date_size - t) % date_size
        spot = PLACE[o]
        first, size, land = taken[o]
        if kind == 0 and t == 0:
            src = image_hbm.at[:, 0, pl.ds(lines - FINE if o == 1 else 0, FINE), :]
            dst = margin.at[0 if o == 1 else 1]
        elif kind == 2:
            skip = 0 if o == 1 else FINE
            src = tile.at[:, pl.ds(first + skip, REACH - FINE), :]
            dst = near.at[0, :, pl.ds(land + skip, REACH - FINE), :]
        elif kind == 0:
            src = tile.at[:, pl.ds(first, size), :]
            dst = far.at[slot - 1, :, pl.ds(land, size), :]
        else:
            src, dst = kernels, all_kernels.at[slot, spot]
        return pltpu.make_async_remote_copy(
            src_ref=src, dst_ref=dst,
            send_sem=send_sem.at[t, spot, kind],
            recv_sem=recv_sem.at[slot, spot, kind],
            device_id=target, device_id_type=MESH,
        )

    def push(o, t, kind):
        send(o, t, kind, place_at(o, t)).start()

    pl.semaphore_wait(barrier, has_up.astype(jnp.int32) * (d + 1) + d + 1)
    for o, t in peers:
        if o <= 0:
            @pl.when(jnp.logical_and(wraps[t] if t else True, has_up if o else True))
            def _(o=o, t=t):
                pl.semaphore_signal(
                    ready.at[PLACE[-o], (date_size - t) % date_size], inc=1,
                    device_id=place_at(o, t), device_id_type=MESH)

    leads = jnp.logical_or(d == 0, g == 1)

    @pl.when(jnp.logical_and(has_up, leads))
    def _():
        push(-1, 0, 0)

    for load in loads[:2]:
        load.wait()
    shifts = jnp.broadcast_to(offsets[0:1, :].astype(jnp.float32), (TAPS, lines))
    held = jnp.concatenate([taps[:, 0], shifts], axis=1)
    kernels[...] = held
    all_kernels[0, 1] = held

    @pl.when(jnp.logical_and(has_up, leads))
    def _():
        push(-1, 0, 1)

    loads[2].wait()
    for c in range(2):
        tile[c] = image[c, 0].astype(jnp.bfloat16)
    for t in range(1, date_size):
        @pl.when(wraps[t])
        def _(t=t):
            @pl.when(has_up)
            def _():
                push(-1, t, 1)
                push(-1, t, 0)

            push(0, t, 1)
            push(0, t, 0)

    @pl.when(has_up)
    def _():
        push(-1, 0, 2)

    @pl.when(jnp.logical_and(has_up, jnp.logical_not(leads)))
    def _():
        push(-1, 0, 1)
        push(-1, 0, 0)

    for load in loads[3:]:
        load.start()
    for c in range(2):
        value = image[c, 0]
        high = value.astype(jnp.bfloat16)
        near[0, c, REACH : REACH + lines] = high
        near[1, c, REACH : REACH + lines] = (value - high.astype(jnp.float32)).astype(jnp.bfloat16)

    for t in range(1, date_size):
        @pl.when(jnp.logical_not(wraps[t]))
        def _(t=t):
            pl.semaphore_wait(ready.at[PLACE[0], t], 1)
            push(0, t, 1)
            push(0, t, 0)

            @pl.when(has_up)
            def _():
                push(-1, t, 1)
                push(-1, t, 0)

    @pl.when(has_down)
    def _():
        pl.semaphore_wait(ready.at[PLACE[1], 0], 1)
        for t in range(1, date_size):
            @pl.when(wraps[t])
            def _(t=t):
                push(1, t, 1)
                push(1, t, 0)

        push(1, 0, 1)
        push(1, 0, 0)
        push(1, 0, 2)
        for t in range(1, date_size):
            @pl.when(jnp.logical_not(wraps[t]))
            def _(t=t):
                pl.semaphore_wait(ready.at[PLACE[1], t], 1)
                push(1, t, 1)
                push(1, t, 0)

    def arrived(slot, kinds):
        t = (date_size - slot) % date_size
        for o in (-1, 0, 1):
            if (o, t) != (0, 0):
                def _(o=o):
                    for kind in kinds:
                        send(o, t, kind, place_at(-o, slot)).wait_recv()
                guarded(-o, _)

    def side(slot):
        return pltpu.make_async_remote_copy(
            src_ref=ifg.at[slot, pl.ds(pl.multiple_of(samples - (samples - HALF) * g, HALF), HALF)],
            dst_ref=ifg.at[slot, pl.ds(pl.multiple_of((samples + HALF) * g, HALF), HALF)],
            send_sem=side_sem.at[0, slot], recv_sem=side_sem.at[1, slot],
            device_id=other_core, device_id_type=MESH,
        )

    def side_arrived(slot):
        pltpu.make_async_remote_copy(
            src_ref=ifg.at[slot, pl.ds(pl.multiple_of(samples - (samples - HALF) * g, HALF), HALF)],
            dst_ref=ifg.at[slot, pl.ds(pl.multiple_of((samples + HALF) * (1 - g), HALF), HALF)],
            send_sem=side_sem.at[0, slot], recv_sem=side_sem.at[1, slot],
            device_id=other_core, device_id_type=MESH,
        ).wait_recv()

    span = lines + 2 * REACH
    wide_lines = 4 * HALF
    source = lax.broadcasted_iota(jnp.int32, (span, wide_lines), 0)
    place = lax.broadcasted_iota(jnp.int32, (span, wide_lines), 1)
    distance = (source - place - (RIM - (TAPS // 2 - 1))).astype(jnp.float32)

    def make_band(slot):
        above, own_rows, below = (all_kernels[slot, i] for i in range(3))
        weights = jnp.concatenate(
            [above[:, HALF:lines], own_rows[:, :lines], below[:, :HALF]], axis=1
        )
        shift = jnp.concatenate(
            [above[:, lines + HALF :], own_rows[:, lines:], below[:, lines : lines + HALF]], axis=1
        )
        gap = distance - shift[0:1]
        band = jnp.zeros((span, wide_lines), jnp.float32)
        for k in range(TAPS):
            band = jnp.where(gap == float(k), weights[k : k + 1], band)
        band_high = band.astype(jnp.bfloat16)
        band_low = (band - band_high.astype(jnp.float32)).astype(jnp.bfloat16)
        bands[slot] = jnp.concatenate([band_high, band_low], axis=1)

    def resample(slot, pieces, at, size):
        total = None
        for piece in pieces:
            columns = [piece[c, :, pl.ds(at, size)] for c in range(2)]
            product = lax.dot_general(
                jnp.concatenate(columns, axis=1), bands[slot], (((0,), (0,)), ((), ())),
                preferred_element_type=jnp.float32,
            )
            product = product[:, :wide_lines] + product[:, wide_lines:]
            total = product if total is None else total + product
        total = total.astype(jnp.bfloat16).astype(jnp.float32)
        return total[:size], total[size:]

    def store(slot, at, real_part, imag_part):
        rows = pl.ds(at, real_part.shape[0])
        ifg[slot, rows, :wide_lines] = real_part.astype(jnp.bfloat16)
        ifg[slot, rows, wide_lines:] = imag_part.astype(jnp.bfloat16)

    def take_own():
        arrived(0, (1, 0, 2))
        make_band(0)
        for i in range(2):
            for c in range(2):
                value = margin[i, c]
                high = value.astype(jnp.bfloat16)
                first = REACH - FINE if i == 0 else REACH + lines
                at = slice(first, first + FINE)
                near[0, c, at] = high
                near[1, c, at] = (value - high.astype(jnp.float32)).astype(jnp.bfloat16)
        real, imag = resample(0, [near.at[0], near.at[1]], 0, samples)
        own[0], own[1] = real, imag
        store(0, HALF, real * real + imag * imag, jnp.zeros_like(real))
        side(0).start()

    def take_other(slot):
        arrived(slot, (1,))
        make_band(slot)
        arrived(slot, (0,))
        size = samples // 2
        for i, half in enumerate((1 - g, g)):
            at = pl.multiple_of(half * size, size)
            real, imag = resample(slot, [far.at[slot - 1]], at, size)
            own_real, own_imag = own[0, pl.ds(at, size)], own[1, pl.ds(at, size)]
            store(
                slot, pl.multiple_of(at + HALF, HALF), own_real * real + own_imag * imag,
                own_imag * real - own_real * imag,
            )
            if i == 0:
                side(slot).start()

    take_own()
    for load in loads[3:]:
        load.wait()
    if date_size == 2:
        single = Filter(ifg.at[0], table, True, *kept[3:], *scratch[3:])
        single.lines(single.inside)
        single.samples(single.inner)
    for j in range(1, date_size):
        take_other(j)
    if date_size == 2:
        cross = Filter(ifg.at[1], table, False, *kept[:3], *scratch[:3])
        cross.lines(cross.inside)
        cross.samples(cross.inner)
        single.gain(single.inner)
        cross.gain(cross.inner)
        single.samples_back_inner()
        cross.samples_back_inner()
    for j in range(date_size):
        side_arrived(j)

    for o, t in peers:
        def _(o=o, t=t):
            for kind in (1, 0) if t else (1, 0, 2):
                send(o, t, kind, place_at(o, t)).wait_send()
        guarded(o, _)
    for slot in range(date_size):
        side(slot).wait_send()


def filter_kernel(date_size, ifg, table, by_date, *rest):
    alone = date_size == 2
    kept, rest = (rest[:6], rest[6:]) if alone else ([], rest)
    out, results, partner, sem, read_sem, *rest = rest
    kept, scratch = (kept, rest) if alone else (rest[:3], rest[3:])
    matches = out.shape[0]
    d = lax.axis_index("date")
    read = pltpu.make_async_copy(by_date, partner, read_sem)
    read.start()

    def deliver(m, c, spot):
        return pltpu.make_async_copy(
            results.at[spot, pl.ds(c * PATCH, PATCH)], out.at[m, c, 0], sem.at[m, c])

    if alone:
        results[0, PATCH:] = jnp.zeros((PATCH, results.shape[2]), results.dtype)
        results[1], results[0, :PATCH] = run_outer(
            Filter(ifg.at[1], table, False, *kept[:3], *scratch[:3]),
            Filter(ifg.at[0], table, True, *kept[3:], *scratch[3:]),
        )
        read.wait()
        for m in range(matches):
            spot = lax.rem(partner[d, m] - d + date_size, date_size)
            for c in range(2):
                deliver(m, c, spot).start()
    else:
        read.wait()
        for m in range(matches):
            spot = lax.rem(partner[d, m] - d + date_size, date_size)
            one = Filter(ifg.at[spot], table, False, *kept, *scratch)
            run_inner(one)
            results[m] = run_outer(one)[0]
            for c in range(2):
                deliver(m, c, m).start()
    for m in range(matches):
        for c in range(2):
            deliver(m, c, 0).wait()


def per_device(az_size, date_size, image_stack, tap_weights, offsets, matchings):
    lines, samples = image_stack.shape[2:]
    assert image_stack.shape[1] == 1 and lines == PATCH
    matches = matchings.shape[0]
    hbm = pl.BlockSpec(memory_space=pltpu.HBM)
    vmem = pl.BlockSpec(memory_space=pltpu.VMEM)
    constants = tables()
    alone = date_size == 2
    passed = [
        pltpu.VMEM((date_size, samples + 2 * HALF, 8 * HALF), jnp.bfloat16),
        pltpu.VMEM(constants.shape, jnp.bfloat16),
        pltpu.VMEM((date_size, matches), jnp.int32),
    ]
    if alone:
        passed += kept_of_filter(samples, LANES) + kept_of_filter(samples, HALF_LANES)
    scratch = scratch_of_filter(samples, LANES)
    if alone:
        scratch += scratch_of_filter(samples, HALF_LANES)
    else:
        scratch = kept_of_filter(samples, LANES) + scratch
    passed = pl.pallas_call(
        functools.partial(stack_kernel, az_size, date_size),
        out_shape=passed,
        in_specs=[hbm] * 5,
        out_specs=[vmem] * len(passed),
        scratch_shapes=(scratch if alone else []) + [
            pltpu.VMEM(image_stack.shape, jnp.float32),
            pltpu.VMEM(tap_weights.shape, jnp.float32),
            pltpu.VMEM(offsets.shape, jnp.int32),
            pltpu.VMEM((2, lines, samples), jnp.bfloat16),
            pltpu.VMEM((TAPS, 2 * lines), jnp.float32),
            pltpu.VMEM((2, 2, lines + 2 * REACH, samples), jnp.bfloat16),
            pltpu.VMEM((date_size - 1, 2, lines + 2 * REACH, samples), jnp.bfloat16),
            pltpu.VMEM((2, 2, FINE, samples), jnp.float32),
            pltpu.VMEM((date_size, 3, TAPS, 2 * lines), jnp.float32),
            pltpu.VMEM((date_size, lines + 2 * REACH, 8 * HALF), jnp.bfloat16),
            pltpu.VMEM((2, samples, 4 * HALF), jnp.float32),
            pltpu.SemaphoreType.DMA((5,)),
            pltpu.SemaphoreType.DMA((date_size, 3, 3)),
            pltpu.SemaphoreType.DMA((date_size, 3, 3)),
            pltpu.SemaphoreType.DMA((2, date_size)),
            pltpu.SemaphoreType.REGULAR((3, date_size)),
        ],
        compiler_params=pltpu.CompilerParams(collective_id=0, has_side_effects=True),
    )(image_stack, tap_weights, offsets, jnp.asarray(constants), matchings.T)
    return pl.pallas_call(
        functools.partial(filter_kernel, date_size),
        out_shape=jax.ShapeDtypeStruct((matches, 2, 1, lines, samples), jnp.float32),
        in_specs=[vmem] * len(passed),
        out_specs=hbm,
        scratch_shapes=[
            pltpu.VMEM((2 if alone else matches, 2 * lines, samples), jnp.float32),
            pltpu.SMEM((date_size, matches), jnp.int32),
            pltpu.SemaphoreType.DMA((matches, 2)),
            pltpu.SemaphoreType.DMA,
        ] + scratch,
        compiler_params=pltpu.CompilerParams(vmem_limit_bytes=24 << 20),
    )(*passed)


def solution(mesh):
    placed = (
        P(None, ("parts", "date"), "az", "rg"),
        P(None, ("parts", "date"), "az"),
        P(("parts", "date"), "az"),
        P(),
    )
    assert mesh.shape["rg"] == 2
    return jax.shard_map(
        functools.partial(per_device, mesh.shape["az"], mesh.shape["date"]),
        mesh=mesh,
        in_specs=placed,
        out_specs=P(None, None, ("parts", "date"), "az", "rg"),
        check_vma=False,
    )
```

```python
import functools
import math

import jax
import jax.numpy as jnp
import ml_dtypes
import numpy as np
from jax import lax
from jax.experimental import pallas as pl
from jax.experimental.pallas import tpu as pltpu
from jax.sharding import PartitionSpec as P

TAPS = 8
SHIFT_MAX = 12
PATCH = 64
HALF = PATCH // 2
RIM = SHIFT_MAX + TAPS // 2
REACH = RIM + HALF
FINE = 16
GROUPS = 4
LANES = GROUPS * PATCH
HALF_LANES = 128
HALF_GROUP = HALF + 3
MESH = pl.DeviceIdType.MESH
BF16 = ml_dtypes.bfloat16
PLACE = {1: 0, 0: 1, -1: 2}


def fourier_table(sine_sign, table_scale):
    ids = np.arange(PATCH)
    angles = ((ids[:, None] * ids[None, :]) % PATCH) * (2.0 * math.pi / PATCH)
    cosine = np.cos(angles) * table_scale
    sine = np.sin(angles) * (sine_sign * table_scale)
    table = np.block([[cosine, -sine], [sine, cosine]]).astype(np.float32)
    return table.astype(BF16).astype(np.float32)


def tables():
    forward = fourier_table(1.0, 1.0)
    inverse = fourier_table(-1.0, 1.0 / PATCH)
    window = np.sin(math.pi * (np.arange(PATCH, dtype=np.float32) + 0.5) / PATCH) ** 2
    wide = 2 * PATCH
    line_in = np.zeros((2, wide, 2, GROUPS, PATCH), np.float32)
    line_out = np.zeros((2, PATCH, 2, GROUPS, PATCH), np.float32)
    real_in = np.zeros((wide, 2, HALF_LANES), np.float32)
    real_out = np.zeros((PATCH, 2, HALF_LANES), np.float32)
    real_ring = np.zeros((HALF_LANES, HALF_LANES), np.float32)
    split_f = forward.reshape(2, PATCH, 2, PATCH)
    split_i = inverse.reshape(2, PATCH, 2, PATCH)
    for r in range(3):
        line_in[:, r * HALF : r * HALF + PATCH, :, r] = split_f
        for at in range(HALF_GROUP):
            f, lane = (at - 1) % PATCH, r * HALF_GROUP + at
            real_in[r * HALF : r * HALF + PATCH, :, lane] = split_f[0, :, :, f]
            if 0 < at < HALF_GROUP - 1:
                real_ring[lane - 1 : lane + 2, lane] = 1.0
        for line in range(PATCH):
            u = line + HALF - HALF * r
            if 0 <= u < PATCH:
                line_out[:, line, :, r] = split_i[:, :, :, u].transpose(2, 0, 1) * window[u]
                for at in range(1, HALF_GROUP - 1):
                    f = at - 1
                    times = 1.0 if f in (0, HALF) else 2.0
                    real_out[line, :, r * HALF_GROUP + at] = split_i[:, f, 0, u] * window[u] * times
    line_in = line_in.reshape(2 * wide, 2 * LANES).astype(BF16)
    line_out = line_out.reshape(wide, 2 * LANES)
    high = line_out.astype(BF16)
    low = (line_out - high.astype(np.float32)).astype(BF16)
    ids = np.arange(LANES)
    gap = (ids[:, None] - ids[None, :]) % PATCH
    same = ids[:, None] // PATCH == ids[None, :] // PATCH
    ring = (((gap <= 1) | (gap == PATCH - 1)) & same).astype(BF16)
    turns = np.concatenate([forward.T, inverse.T], axis=0).astype(BF16)
    rows = np.broadcast_to(np.tile(window, 2)[:, None], (wide, wide)).astype(np.float32)
    rows_high = rows.astype(BF16)
    rows_low = (rows - rows_high.astype(np.float32)).astype(BF16)
    last = np.concatenate([ring, turns, np.concatenate([rows_high, rows_low], axis=0)], axis=1)
    real_in = real_in.reshape(wide, 2 * HALF_LANES).astype(BF16)
    real_out = real_out.reshape(PATCH, 2 * HALF_LANES)
    real_high = real_out.astype(BF16)
    real_low = (real_out - real_high.astype(np.float32)).astype(BF16)
    real = np.concatenate([real_in, np.concatenate([real_high, real_low], axis=0)], axis=1)
    rest = np.zeros((wide, 2 * LANES), BF16)
    rest[:, :HALF_LANES] = real_ring.astype(BF16)
    return np.concatenate([line_in, high, low, last, real, rest], axis=0)


class Filter:
    def __init__(self, ifg, table, real, spectra, back, edge, spec, power_sum, shaped):
        wide = 2 * PATCH
        self.ifg, self.table = ifg, table
        self.spectra, self.back, self.edge = spectra, back, edge
        self.spec, self.power_sum, self.shaped = spec, power_sum, shaped
        self.depth = (1 if real else 2) * wide
        self.lanes = lanes = HALF_LANES if real else LANES
        columns = spec.shape[0]
        self.inner, self.outer = range(1, columns - 1), (0, columns - 1)
        rows = ifg.shape[0]
        self.inside = ((HALF, rows - 2 * HALF),)
        self.outside = ((0, HALF), (rows - HALF, HALF))
        self.line_in = table[6 * wide : 7 * wide, 0:LANES] if real else table[0 : 2 * wide]
        self.ring = table[7 * wide :, 0:lanes] if real else table[4 * wide : 6 * wide, 0:LANES]
        self.line_out = table[6 * wide : 7 * wide, LANES:] if real else table[2 * wide : 4 * wide]
        self.forward = table[4 * wide : 5 * wide, LANES : LANES + wide]
        self.inverse = table[5 * wide : 6 * wide, LANES : LANES + wide]

    def lines(self, pieces):
        rows = [self.ifg[first : first + size, : self.depth] for first, size in pieces]
        rows = rows[0] if len(rows) == 1 else jnp.concatenate(rows, axis=0)
        made = jnp.dot(rows, self.line_in, preferred_element_type=jnp.float32)
        made, at = made.astype(jnp.bfloat16), 0
        for first, size in pieces:
            self.spectra[first : first + size] = made[at : at + size]
            at += size

    def samples(self, which):
        for q in which:
            rows = self.spectra[q * HALF : q * HALF + PATCH]
            block = jnp.concatenate([rows[:, : self.lanes], rows[:, self.lanes :]], axis=0)
            spectrum = jnp.dot(self.forward, block, preferred_element_type=jnp.float32)
            self.spec[q] = spectrum
            re, im = spectrum[:PATCH], spectrum[PATCH:]
            power = re * re + im * im
            summed = power + pltpu.roll(power, 1, 0) + pltpu.roll(power, PATCH - 1, 0)
            self.power_sum[q * PATCH : (q + 1) * PATCH] = summed.astype(jnp.bfloat16)

    def gain(self, which):
        if len(which) == 2:
            power = jnp.concatenate(
                [self.power_sum[q * PATCH : (q + 1) * PATCH] for q in which], axis=0)
        else:
            power = self.power_sum[which[0] * PATCH : (which[-1] + 1) * PATCH]
        smooth = jnp.dot(power, self.ring, preferred_element_type=jnp.float32)
        gains = lax.rsqrt(lax.rsqrt(1.0 + smooth * (1.0 / (9.0 * PATCH * PATCH))))
        for i, q in enumerate(which):
            gain = gains[i * PATCH : (i + 1) * PATCH]
            self.shaped[q, :PATCH] = (self.spec[q, :PATCH] * gain).astype(jnp.bfloat16)
            self.shaped[q, PATCH:] = (self.spec[q, PATCH:] * gain).astype(jnp.bfloat16)

    def ranged(self, which):
        wide = 2 * PATCH
        pieces = [
            self.table[i * wide : (i + 1) * wide, LANES + wide : LANES + 2 * wide].astype(
                jnp.float32)
            for i in (4, 5)
        ]
        weights = jnp.concatenate([pieces[0] + pieces[1]] * (self.lanes // wide), axis=1)
        for q in which:
            value = jnp.dot(
                self.inverse, self.shaped[q], preferred_element_type=jnp.float32) * weights
            yield q, [[value[c * PATCH + i * HALF : c * PATCH + (i + 1) * HALF]
                       for c in range(2)] for i in range(2)]

    def join(self, j, second, first):
        for c in range(2):
            self.back[j * HALF : (j + 1) * HALF, c * self.lanes : (c + 1) * self.lanes] = (
                (second[c] + first[c]).astype(jnp.bfloat16))

    def samples_back_inner(self):
        held = None
        for q, halves in self.ranged(self.inner):
            if held is None:
                self.edge[0, 0], self.edge[0, 1] = halves[0]
            else:
                self.join(q - 1, held, halves[0])
            held = halves[1]
        self.edge[1, 0], self.edge[1, 1] = held

    def samples_back_outer(self):
        (_, left), (last, right) = self.ranged(self.outer)
        self.join(0, left[1], [self.edge[0, 0], self.edge[0, 1]])
        self.join(last - 1, [self.edge[1, 0], self.edge[1, 1]], right[0])

    def lines_back(self):
        split = lax.dot_general(
            self.line_out, self.back[...], (((1,), (1,)), ((), ())),
            preferred_element_type=jnp.float32,
        )
        tall = split.shape[0] // 2
        return split[:tall] + split[tall:]


def run_inner(*filters):
    for one in filters:
        one.lines(one.inside)
    for one in filters:
        one.samples(one.inner)
    for one in filters:
        one.gain(one.inner)
    for one in filters:
        one.samples_back_inner()


def run_outer(*filters):
    for one in filters:
        one.lines(one.outside)
    for one in filters:
        one.samples(one.outer)
    for one in filters:
        one.gain(one.outer)
    for one in filters:
        one.samples_back_outer()
    return [one.lines_back() for one in filters]


def kept_of_filter(samples, lanes):
    return [
        pltpu.VMEM((samples + 2 * HALF, 2 * lanes), jnp.bfloat16),
        pltpu.VMEM((samples, 2 * lanes), jnp.bfloat16),
        pltpu.VMEM((2, 2, HALF, lanes), jnp.float32),
    ]


def scratch_of_filter(samples, lanes):
    columns = samples // HALF + 1
    return [
        pltpu.VMEM((columns, 2 * PATCH, lanes), jnp.float32),
        pltpu.VMEM((columns * PATCH, lanes), jnp.bfloat16),
        pltpu.VMEM((columns, 2 * PATCH, lanes), jnp.bfloat16),
    ]


def stack_kernel(
    az_size, date_size, image_hbm, taps_hbm, offsets_hbm, table_hbm, by_date, ifg, table, passed,
    *rest,
):
    if date_size == 2:
        kept, scratch, rest = rest[:6], rest[6:12], rest[12:]
    (
        image, taps, offsets, tile, kernels, near, far, margin, all_kernels, bands, own,
        load_sem, send_sem, recv_sem, side_sem, ready,
    ) = rest
    a = lax.axis_index("az")
    d = lax.axis_index("date")
    g = lax.axis_index("rg")
    lines = image.shape[2]
    samples = image.shape[3]
    wide = 2 * PATCH
    loads = [
        pltpu.make_async_copy(source, target, load_sem.at[i])
        for i, (source, target) in enumerate(
            ((offsets_hbm, offsets), (taps_hbm, taps), (image_hbm, image), (table_hbm, table),
             (by_date, passed))
        )
    ]
    has_up = a > 0
    has_down = a < az_size - 1
    exists = {-1: has_up, 0: None, 1: has_down}
    wraps = {t: d + t >= date_size for t in range(date_size)}

    def guarded(step, body):
        if exists[step] is None:
            body()
        else:
            pl.when(exists[step])(body)

    def place_at(az_step, date_step):
        return {"az": a + az_step, "date": lax.rem(d + date_step, date_size), "rg": g}

    other_core = {"az": a, "date": d, "rg": 1 - g}
    peers = [(o, t) for o in (-1, 0, 1) for t in range(date_size) if (o, t) != (0, 0)]

    barrier = pltpu.get_barrier_semaphore()
    pl.semaphore_signal(barrier, inc=1, device_id=other_core, device_id_type=MESH)
    for o, t in peers:
        if o >= 0:
            @pl.when(jnp.logical_and(jnp.logical_not(wraps[t]), has_down if o else True))
            def _(o=o, t=t):
                pl.semaphore_signal(barrier, inc=1, device_id=place_at(o, t), device_id_type=MESH)
    for load in loads[:3]:
        load.start()

    coarse = jnp.zeros((2, REACH - FINE, samples), near.dtype)
    near[1, :, 0 : REACH - FINE] = coarse
    near[1, :, REACH + lines + FINE :] = coarse

    @pl.when(jnp.logical_not(has_up))
    def _():
        near[0, :, 0 : REACH - FINE] = coarse
        margin[0] = jnp.zeros(margin.shape[1:], margin.dtype)
        far[:, :, 0:REACH] = jnp.zeros((date_size - 1, 2, REACH, samples), far.dtype)
        all_kernels[:, 0] = jnp.zeros((date_size,) + all_kernels.shape[2:], jnp.float32)

    @pl.when(jnp.logical_not(has_down))
    def _():
        near[0, :, REACH + lines + FINE :] = coarse
        margin[1] = jnp.zeros(margin.shape[1:], margin.dtype)
        far[:, :, REACH + lines :] = jnp.zeros((date_size - 1, 2, REACH, samples), far.dtype)
        all_kernels[:, 2] = jnp.zeros((date_size,) + all_kernels.shape[2:], jnp.float32)

    no_side = jnp.zeros((date_size, HALF, ifg.shape[2]), ifg.dtype)

    @pl.when(g == 0)
    def _():
        ifg[:, 0:HALF] = no_side

    @pl.when(g != 0)
    def _():
        ifg[:, HALF + samples :] = no_side

    taken = {
        1: (lines - REACH, REACH, 0), 0: (0, lines, REACH), -1: (0, REACH, REACH + lines),
    }

    def send(o, t, kind, target):
        slot = (date_size - t) % date_size
        spot = PLACE[o]
        first, size, land = taken[o]
        if kind == 0 and t == 0:
            src = image_hbm.at[:, 0, pl.ds(lines - FINE if o == 1 else 0, FINE), :]
            dst = margin.at[0 if o == 1 else 1]
        elif kind == 2:
            skip = 0 if o == 1 else FINE
            src = tile.at[:, pl.ds(first + skip, REACH - FINE), :]
            dst = near.at[0, :, pl.ds(land + skip, REACH - FINE), :]
        elif kind == 0:
            src = tile.at[:, pl.ds(first, size), :]
            dst = far.at[slot - 1, :, pl.ds(land, size), :]
        else:
            src, dst = kernels, all_kernels.at[slot, spot]
        return pltpu.make_async_remote_copy(
            src_ref=src, dst_ref=dst,
            send_sem=send_sem.at[t, spot, kind],
            recv_sem=recv_sem.at[slot, spot, kind],
            device_id=target, device_id_type=MESH,
        )

    def push(o, t, kind):
        send(o, t, kind, place_at(o, t)).start()

    pl.semaphore_wait(barrier, has_up.astype(jnp.int32) * (d + 1) + d + 1)
    for o, t in peers:
        if o <= 0:
            @pl.when(jnp.logical_and(wraps[t] if t else True, has_up if o else True))
            def _(o=o, t=t):
                pl.semaphore_signal(
                    ready.at[PLACE[-o], (date_size - t) % date_size], inc=1,
                    device_id=place_at(o, t), device_id_type=MESH)

    leads = jnp.logical_or(d == 0, g == 1)

    @pl.when(jnp.logical_and(has_up, leads))
    def _():
        push(-1, 0, 0)

    for load in loads[:2]:
        load.wait()
    shifts = jnp.broadcast_to(offsets[0:1, :].astype(jnp.float32), (TAPS, lines))
    held = jnp.concatenate([taps[:, 0], shifts], axis=1)
    kernels[...] = held
    all_kernels[0, 1] = held

    @pl.when(jnp.logical_and(has_up, leads))
    def _():
        push(-1, 0, 1)

    loads[2].wait()
    for c in range(2):
        tile[c] = image[c, 0].astype(jnp.bfloat16)
    for t in range(1, date_size):
        @pl.when(wraps[t])
        def _(t=t):
            @pl.when(has_up)
            def _():
                push(-1, t, 1)
                push(-1, t, 0)

            push(0, t, 1)
            push(0, t, 0)

    @pl.when(has_up)
    def _():
        push(-1, 0, 2)

    @pl.when(jnp.logical_and(has_up, jnp.logical_not(leads)))
    def _():
        push(-1, 0, 1)
        push(-1, 0, 0)

    for load in loads[3:]:
        load.start()
    for c in range(2):
        value = image[c, 0]
        high = value.astype(jnp.bfloat16)
        near[0, c, REACH : REACH + lines] = high
        near[1, c, REACH : REACH + lines] = (value - high.astype(jnp.float32)).astype(jnp.bfloat16)

    for t in range(1, date_size):
        @pl.when(jnp.logical_not(wraps[t]))
        def _(t=t):
            pl.semaphore_wait(ready.at[PLACE[0], t], 1)
            @pl.when(has_up)
            def _():
                push(-1, t, 1)
                push(-1, t, 0)

            push(0, t, 1)
            push(0, t, 0)

    @pl.when(has_down)
    def _():
        pl.semaphore_wait(ready.at[PLACE[1], 0], 1)
        for t in range(1, date_size):
            @pl.when(wraps[t])
            def _(t=t):
                push(1, t, 1)
                push(1, t, 0)

        push(1, 0, 1)
        push(1, 0, 0)
        push(1, 0, 2)
        for t in range(1, date_size):
            @pl.when(jnp.logical_not(wraps[t]))
            def _(t=t):
                pl.semaphore_wait(ready.at[PLACE[1], t], 1)
                push(1, t, 1)
                push(1, t, 0)

    def arrived(slot, kinds):
        t = (date_size - slot) % date_size
        for o in (-1, 0, 1):
            if (o, t) != (0, 0):
                def _(o=o):
                    for kind in kinds:
                        send(o, t, kind, place_at(-o, slot)).wait_recv()
                guarded(-o, _)

    def side(slot):
        return pltpu.make_async_remote_copy(
            src_ref=ifg.at[slot, pl.ds(pl.multiple_of(samples - (samples - HALF) * g, HALF), HALF)],
            dst_ref=ifg.at[slot, pl.ds(pl.multiple_of((samples + HALF) * g, HALF), HALF)],
            send_sem=side_sem.at[0, slot], recv_sem=side_sem.at[1, slot],
            device_id=other_core, device_id_type=MESH,
        )

    def side_arrived(slot):
        pltpu.make_async_remote_copy(
            src_ref=ifg.at[slot, pl.ds(pl.multiple_of(samples - (samples - HALF) * g, HALF), HALF)],
            dst_ref=ifg.at[slot, pl.ds(pl.multiple_of((samples + HALF) * (1 - g), HALF), HALF)],
            send_sem=side_sem.at[0, slot], recv_sem=side_sem.at[1, slot],
            device_id=other_core, device_id_type=MESH,
        ).wait_recv()

    span = lines + 2 * REACH
    wide_lines = 4 * HALF
    source = lax.broadcasted_iota(jnp.int32, (span, wide_lines), 0)
    place = lax.broadcasted_iota(jnp.int32, (span, wide_lines), 1)
    distance = (source - place - (RIM - (TAPS // 2 - 1))).astype(jnp.float32)

    def make_band(slot):
        above, own_rows, below = (all_kernels[slot, i] for i in range(3))
        weights = jnp.concatenate(
            [above[:, HALF:lines], own_rows[:, :lines], below[:, :HALF]], axis=1
        )
        shift = jnp.concatenate(
            [above[:, lines + HALF :], own_rows[:, lines:], below[:, lines : lines + HALF]], axis=1
        )
        gap = distance - shift[0:1]
        band = jnp.zeros((span, wide_lines), jnp.float32)
        for k in range(TAPS):
            band = jnp.where(gap == float(k), weights[k : k + 1], band)
        band_high = band.astype(jnp.bfloat16)
        band_low = (band - band_high.astype(jnp.float32)).astype(jnp.bfloat16)
        bands[slot] = jnp.concatenate([band_high, band_low], axis=1)

    def resample(slot, pieces, at, size):
        total = None
        for piece in pieces:
            columns = [piece[c, :, pl.ds(at, size)] for c in range(2)]
            product = lax.dot_general(
                jnp.concatenate(columns, axis=1), bands[slot], (((0,), (0,)), ((), ())),
                preferred_element_type=jnp.float32,
            )
            product = product[:, :wide_lines] + product[:, wide_lines:]
            total = product if total is None else total + product
        total = total.astype(jnp.bfloat16).astype(jnp.float32)
        return total[:size], total[size:]

    def store(slot, at, real_part, imag_part):
        rows = pl.ds(at, real_part.shape[0])
        ifg[slot, rows, :wide_lines] = real_part.astype(jnp.bfloat16)
        ifg[slot, rows, wide_lines:] = imag_part.astype(jnp.bfloat16)

    def take_own():
        arrived(0, (1, 0, 2))
        make_band(0)
        for i in range(2):
            for c in range(2):
                value = margin[i, c]
                high = value.astype(jnp.bfloat16)
                first = REACH - FINE if i == 0 else REACH + lines
                at = slice(first, first + FINE)
                near[0, c, at] = high
                near[1, c, at] = (value - high.astype(jnp.float32)).astype(jnp.bfloat16)
        real, imag = resample(0, [near.at[0], near.at[1]], 0, samples)
        own[0], own[1] = real, imag
        store(0, HALF, real * real + imag * imag, jnp.zeros_like(real))
        side(0).start()

    def take_other(slot):
        arrived(slot, (1,))
        make_band(slot)
        arrived(slot, (0,))
        size = samples // 2
        for i, half in enumerate((1 - g, g)):
            at = pl.multiple_of(half * size, size)
            real, imag = resample(slot, [far.at[slot - 1]], at, size)
            own_real, own_imag = own[0, pl.ds(at, size)], own[1, pl.ds(at, size)]
            store(
                slot, pl.multiple_of(at + HALF, HALF), own_real * real + own_imag * imag,
                own_imag * real - own_real * imag,
            )
            if i == 0:
                side(slot).start()

    take_own()
    for load in loads[3:]:
        load.wait()
    if date_size == 2:
        single = Filter(ifg.at[0], table, True, *kept[3:], *scratch[3:])
        single.lines(single.inside)
        single.samples(single.inner)
    for j in range(1, date_size):
        take_other(j)
    if date_size == 2:
        cross = Filter(ifg.at[1], table, False, *kept[:3], *scratch[:3])
        cross.lines(cross.inside)
        cross.samples(cross.inner)
        single.gain(single.inner)
        cross.gain(cross.inner)
        single.samples_back_inner()
        cross.samples_back_inner()
    for o, t in peers:
        def _(o=o, t=t):
            for kind in (1, 0) if t else (1, 0, 2):
                send(o, t, kind, place_at(o, t)).wait_send()
        guarded(o, _)
    for j in range(date_size):
        side_arrived(j)
    for slot in range(date_size):
        side(slot).wait_send()


def filter_kernel(date_size, ifg, table, by_date, *rest):
    alone = date_size == 2
    kept, rest = (rest[:6], rest[6:]) if alone else ([], rest)
    out, results, partner, sem, read_sem, *rest = rest
    kept, scratch = (kept, rest) if alone else (rest[:3], rest[3:])
    matches = out.shape[0]
    d = lax.axis_index("date")
    read = pltpu.make_async_copy(by_date, partner, read_sem)
    read.start()

    def deliver(m, c, spot):
        return pltpu.make_async_copy(
            results.at[spot, pl.ds(c * PATCH, PATCH)], out.at[m, c, 0], sem.at[m, c])

    if alone:
        results[0, PATCH:] = jnp.zeros((PATCH, results.shape[2]), results.dtype)
        results[1], results[0, :PATCH] = run_outer(
            Filter(ifg.at[1], table, False, *kept[:3], *scratch[:3]),
            Filter(ifg.at[0], table, True, *kept[3:], *scratch[3:]),
        )
        read.wait()
        for m in range(matches):
            spot = lax.rem(partner[d, m] - d + date_size, date_size)
            for c in range(2):
                deliver(m, c, spot).start()
    else:
        read.wait()
        for m in range(matches):
            spot = lax.rem(partner[d, m] - d + date_size, date_size)
            one = Filter(ifg.at[spot], table, False, *kept, *scratch)
            run_inner(one)
            results[m] = run_outer(one)[0]
            for c in range(2):
                deliver(m, c, m).start()
    for m in range(matches):
        for c in range(2):
            deliver(m, c, 0).wait()


def per_device(az_size, date_size, image_stack, tap_weights, offsets, matchings):
    lines, samples = image_stack.shape[2:]
    assert image_stack.shape[1] == 1 and lines == PATCH
    matches = matchings.shape[0]
    hbm = pl.BlockSpec(memory_space=pltpu.HBM)
    vmem = pl.BlockSpec(memory_space=pltpu.VMEM)
    constants = tables()
    alone = date_size == 2
    passed = [
        pltpu.VMEM((date_size, samples + 2 * HALF, 8 * HALF), jnp.bfloat16),
        pltpu.VMEM(constants.shape, jnp.bfloat16),
        pltpu.VMEM((date_size, matches), jnp.int32),
    ]
    if alone:
        passed += kept_of_filter(samples, LANES) + kept_of_filter(samples, HALF_LANES)
    scratch = scratch_of_filter(samples, LANES)
    if alone:
        scratch += scratch_of_filter(samples, HALF_LANES)
    else:
        scratch = kept_of_filter(samples, LANES) + scratch
    passed = pl.pallas_call(
        functools.partial(stack_kernel, az_size, date_size),
        out_shape=passed,
        in_specs=[hbm] * 5,
        out_specs=[vmem] * len(passed),
        scratch_shapes=(scratch if alone else []) + [
            pltpu.VMEM(image_stack.shape, jnp.float32),
            pltpu.VMEM(tap_weights.shape, jnp.float32),
            pltpu.VMEM(offsets.shape, jnp.int32),
            pltpu.VMEM((2, lines, samples), jnp.bfloat16),
            pltpu.VMEM((TAPS, 2 * lines), jnp.float32),
            pltpu.VMEM((2, 2, lines + 2 * REACH, samples), jnp.bfloat16),
            pltpu.VMEM((date_size - 1, 2, lines + 2 * REACH, samples), jnp.bfloat16),
            pltpu.VMEM((2, 2, FINE, samples), jnp.float32),
            pltpu.VMEM((date_size, 3, TAPS, 2 * lines), jnp.float32),
            pltpu.VMEM((date_size, lines + 2 * REACH, 8 * HALF), jnp.bfloat16),
            pltpu.VMEM((2, samples, 4 * HALF), jnp.float32),
            pltpu.SemaphoreType.DMA((5,)),
            pltpu.SemaphoreType.DMA((date_size, 3, 3)),
            pltpu.SemaphoreType.DMA((date_size, 3, 3)),
            pltpu.SemaphoreType.DMA((2, date_size)),
            pltpu.SemaphoreType.REGULAR((3, date_size)),
        ],
        compiler_params=pltpu.CompilerParams(collective_id=0, has_side_effects=True),
    )(image_stack, tap_weights, offsets, jnp.asarray(constants), matchings.T)
    return pl.pallas_call(
        functools.partial(filter_kernel, date_size),
        out_shape=jax.ShapeDtypeStruct((matches, 2, 1, lines, samples), jnp.float32),
        in_specs=[vmem] * len(passed),
        out_specs=hbm,
        scratch_shapes=[
            pltpu.VMEM((2 if alone else matches, 2 * lines, samples), jnp.float32),
            pltpu.SMEM((date_size, matches), jnp.int32),
            pltpu.SemaphoreType.DMA((matches, 2)),
            pltpu.SemaphoreType.DMA,
        ] + scratch,
        compiler_params=pltpu.CompilerParams(vmem_limit_bytes=24 << 20),
    )(*passed)


def solution(mesh):
    placed = (
        P(None, ("parts", "date"), "az", "rg"),
        P(None, ("parts", "date"), "az"),
        P(("parts", "date"), "az"),
        P(),
    )
    assert mesh.shape["rg"] == 2
    return jax.shard_map(
        functools.partial(per_device, mesh.shape["az"], mesh.shape["date"]),
        mesh=mesh,
        in_specs=placed,
        out_specs=P(None, None, ("parts", "date"), "az", "rg"),
        check_vma=False,
    )
```

```python
import functools
import math

import jax
import jax.numpy as jnp
import ml_dtypes
import numpy as np
from jax import lax
from jax.experimental import pallas as pl
from jax.experimental.pallas import tpu as pltpu
from jax.sharding import PartitionSpec as P

TAPS = 8
SHIFT_MAX = 12
PATCH = 64
HALF = PATCH // 2
RIM = SHIFT_MAX + TAPS // 2
REACH = RIM + HALF
FINE = 16
GROUPS = 4
LANES = GROUPS * PATCH
HALF_LANES = 128
HALF_GROUP = HALF + 3
MESH = pl.DeviceIdType.MESH
BF16 = ml_dtypes.bfloat16
PLACE = {1: 0, 0: 1, -1: 2}


def fourier_table(sine_sign, table_scale):
    ids = np.arange(PATCH)
    angles = ((ids[:, None] * ids[None, :]) % PATCH) * (2.0 * math.pi / PATCH)
    cosine = np.cos(angles) * table_scale
    sine = np.sin(angles) * (sine_sign * table_scale)
    table = np.block([[cosine, -sine], [sine, cosine]]).astype(np.float32)
    return table.astype(BF16).astype(np.float32)


def tables():
    forward = fourier_table(1.0, 1.0)
    inverse = fourier_table(-1.0, 1.0 / PATCH)
    window = np.sin(math.pi * (np.arange(PATCH, dtype=np.float32) + 0.5) / PATCH) ** 2
    wide = 2 * PATCH
    line_in = np.zeros((2, wide, 2, GROUPS, PATCH), np.float32)
    line_out = np.zeros((2, PATCH, 2, GROUPS, PATCH), np.float32)
    real_in = np.zeros((wide, 2, HALF_LANES), np.float32)
    real_out = np.zeros((PATCH, 2, HALF_LANES), np.float32)
    real_ring = np.zeros((HALF_LANES, HALF_LANES), np.float32)
    split_f = forward.reshape(2, PATCH, 2, PATCH)
    split_i = inverse.reshape(2, PATCH, 2, PATCH)
    for r in range(3):
        line_in[:, r * HALF : r * HALF + PATCH, :, r] = split_f
        for at in range(HALF_GROUP):
            f, lane = (at - 1) % PATCH, r * HALF_GROUP + at
            real_in[r * HALF : r * HALF + PATCH, :, lane] = split_f[0, :, :, f]
            if 0 < at < HALF_GROUP - 1:
                real_ring[lane - 1 : lane + 2, lane] = 1.0
        for line in range(PATCH):
            u = line + HALF - HALF * r
            if 0 <= u < PATCH:
                line_out[:, line, :, r] = split_i[:, :, :, u].transpose(2, 0, 1) * window[u]
                for at in range(1, HALF_GROUP - 1):
                    f = at - 1
                    times = 1.0 if f in (0, HALF) else 2.0
                    real_out[line, :, r * HALF_GROUP + at] = split_i[:, f, 0, u] * window[u] * times
    line_in = line_in.reshape(2 * wide, 2 * LANES).astype(BF16)
    line_out = line_out.reshape(wide, 2 * LANES)
    high = line_out.astype(BF16)
    low = (line_out - high.astype(np.float32)).astype(BF16)
    ids = np.arange(LANES)
    gap = (ids[:, None] - ids[None, :]) % PATCH
    same = ids[:, None] // PATCH == ids[None, :] // PATCH
    ring = (((gap <= 1) | (gap == PATCH - 1)) & same).astype(BF16)
    turns = np.concatenate([forward.T, inverse.T], axis=0).astype(BF16)
    rows = np.broadcast_to(np.tile(window, 2)[:, None], (wide, wide)).astype(np.float32)
    rows_high = rows.astype(BF16)
    rows_low = (rows - rows_high.astype(np.float32)).astype(BF16)
    last = np.concatenate([ring, turns, np.concatenate([rows_high, rows_low], axis=0)], axis=1)
    real_in = real_in.reshape(wide, 2 * HALF_LANES).astype(BF16)
    real_out = real_out.reshape(PATCH, 2 * HALF_LANES)
    real_high = real_out.astype(BF16)
    real_low = (real_out - real_high.astype(np.float32)).astype(BF16)
    real = np.concatenate([real_in, np.concatenate([real_high, real_low], axis=0)], axis=1)
    rest = np.zeros((wide, 2 * LANES), BF16)
    rest[:, :HALF_LANES] = real_ring.astype(BF16)
    return np.concatenate([line_in, high, low, last, real, rest], axis=0)


class Filter:
    def __init__(self, ifg, table, real, spectra, back, edge, spec, power_sum, shaped):
        wide = 2 * PATCH
        self.ifg, self.table = ifg, table
        self.spectra, self.back, self.edge = spectra, back, edge
        self.spec, self.power_sum, self.shaped = spec, power_sum, shaped
        self.depth = (1 if real else 2) * wide
        self.lanes = lanes = HALF_LANES if real else LANES
        columns = spec.shape[0]
        self.inner, self.outer = range(1, columns - 1), (0, columns - 1)
        rows = ifg.shape[0]
        self.inside = ((HALF, rows - 2 * HALF),)
        self.outside = ((0, HALF), (rows - HALF, HALF))
        self.line_in = table[6 * wide : 7 * wide, 0:LANES] if real else table[0 : 2 * wide]
        self.ring = table[7 * wide :, 0:lanes] if real else table[4 * wide : 6 * wide, 0:LANES]
        self.line_out = table[6 * wide : 7 * wide, LANES:] if real else table[2 * wide : 4 * wide]
        self.forward = table[4 * wide : 5 * wide, LANES : LANES + wide]
        self.inverse = table[5 * wide : 6 * wide, LANES : LANES + wide]

    def lines(self, pieces):
        rows = [self.ifg[first : first + size, : self.depth] for first, size in pieces]
        rows = rows[0] if len(rows) == 1 else jnp.concatenate(rows, axis=0)
        made = jnp.dot(rows, self.line_in, preferred_element_type=jnp.float32)
        made, at = made.astype(jnp.bfloat16), 0
        for first, size in pieces:
            self.spectra[first : first + size] = made[at : at + size]
            at += size

    def samples(self, which):
        for q in which:
            rows = self.spectra[q * HALF : q * HALF + PATCH]
            block = jnp.concatenate([rows[:, : self.lanes], rows[:, self.lanes :]], axis=0)
            spectrum = jnp.dot(self.forward, block, preferred_element_type=jnp.float32)
            self.spec[q] = spectrum
            re, im = spectrum[:PATCH], spectrum[PATCH:]
            power = re * re + im * im
            summed = power + pltpu.roll(power, 1, 0) + pltpu.roll(power, PATCH - 1, 0)
            self.power_sum[q * PATCH : (q + 1) * PATCH] = summed.astype(jnp.bfloat16)

    def gain(self, which):
        if len(which) == 2:
            power = jnp.concatenate(
                [self.power_sum[q * PATCH : (q + 1) * PATCH] for q in which], axis=0)
        else:
            power = self.power_sum[which[0] * PATCH : (which[-1] + 1) * PATCH]
        smooth = jnp.dot(power, self.ring, preferred_element_type=jnp.float32)
        gains = lax.rsqrt(lax.rsqrt(1.0 + smooth * (1.0 / (9.0 * PATCH * PATCH))))
        for i, q in enumerate(which):
            gain = gains[i * PATCH : (i + 1) * PATCH]
            self.shaped[q, :PATCH] = (self.spec[q, :PATCH] * gain).astype(jnp.bfloat16)
            self.shaped[q, PATCH:] = (self.spec[q, PATCH:] * gain).astype(jnp.bfloat16)

    def ranged(self, which):
        wide = 2 * PATCH
        pieces = [
            self.table[i * wide : (i + 1) * wide, LANES + wide : LANES + 2 * wide].astype(
                jnp.float32)
            for i in (4, 5)
        ]
        weights = jnp.concatenate([pieces[0] + pieces[1]] * (self.lanes // wide), axis=1)
        for q in which:
            value = jnp.dot(
                self.inverse, self.shaped[q], preferred_element_type=jnp.float32) * weights
            yield q, [[value[c * PATCH + i * HALF : c * PATCH + (i + 1) * HALF]
                       for c in range(2)] for i in range(2)]

    def join(self, j, second, first):
        for c in range(2):
            self.back[j * HALF : (j + 1) * HALF, c * self.lanes : (c + 1) * self.lanes] = (
                (second[c] + first[c]).astype(jnp.bfloat16))

    def samples_back_inner(self):
        held = None
        for q, halves in self.ranged(self.inner):
            if held is None:
                self.edge[0, 0], self.edge[0, 1] = halves[0]
            else:
                self.join(q - 1, held, halves[0])
            held = halves[1]
        self.edge[1, 0], self.edge[1, 1] = held

    def samples_back_outer(self):
        (_, left), (last, right) = self.ranged(self.outer)
        self.join(0, left[1], [self.edge[0, 0], self.edge[0, 1]])
        self.join(last - 1, [self.edge[1, 0], self.edge[1, 1]], right[0])

    def lines_back(self):
        split = lax.dot_general(
            self.line_out, self.back[...], (((1,), (1,)), ((), ())),
            preferred_element_type=jnp.float32,
        )
        tall = split.shape[0] // 2
        return split[:tall] + split[tall:]


def run_inner(*filters):
    for one in filters:
        one.lines(one.inside)
    for one in filters:
        one.samples(one.inner)
    for one in filters:
        one.gain(one.inner)
    for one in filters:
        one.samples_back_inner()


def run_outer(*filters):
    for one in filters:
        one.lines(one.outside)
    return finish_outer(*filters)


def finish_outer(*filters):
    for one in filters:
        one.samples(one.outer)
    for one in filters:
        one.gain(one.outer)
    for one in filters:
        one.samples_back_outer()
    return [one.lines_back() for one in filters]


def kept_of_filter(samples, lanes):
    return [
        pltpu.VMEM((samples + 2 * HALF, 2 * lanes), jnp.bfloat16),
        pltpu.VMEM((samples, 2 * lanes), jnp.bfloat16),
        pltpu.VMEM((2, 2, HALF, lanes), jnp.float32),
    ]


def scratch_of_filter(samples, lanes):
    columns = samples // HALF + 1
    return [
        pltpu.VMEM((columns, 2 * PATCH, lanes), jnp.float32),
        pltpu.VMEM((columns * PATCH, lanes), jnp.bfloat16),
        pltpu.VMEM((columns, 2 * PATCH, lanes), jnp.bfloat16),
    ]


def stack_kernel(
    az_size, date_size, image_hbm, taps_hbm, offsets_hbm, table_hbm, by_date, ifg, table, passed,
    *rest,
):
    if date_size == 2:
        kept, scratch, rest = rest[:7], rest[7:12], rest[12:]
    (
        image, taps, offsets, tile, kernels, near, far, margin, all_kernels, bands, own,
        load_sem, send_sem, recv_sem, side_sem, ready,
    ) = rest
    a = lax.axis_index("az")
    d = lax.axis_index("date")
    g = lax.axis_index("rg")
    lines = image.shape[2]
    samples = image.shape[3]
    wide = 2 * PATCH
    loads = [
        pltpu.make_async_copy(source, target, load_sem.at[i])
        for i, (source, target) in enumerate(
            ((offsets_hbm, offsets), (taps_hbm, taps), (image_hbm, image), (table_hbm, table),
             (by_date, passed))
        )
    ]
    has_up = a > 0
    has_down = a < az_size - 1
    exists = {-1: has_up, 0: None, 1: has_down}
    wraps = {t: d + t >= date_size for t in range(date_size)}

    def guarded(step, body):
        if exists[step] is None:
            body()
        else:
            pl.when(exists[step])(body)

    def place_at(az_step, date_step):
        return {"az": a + az_step, "date": lax.rem(d + date_step, date_size), "rg": g}

    other_core = {"az": a, "date": d, "rg": 1 - g}
    peers = [(o, t) for o in (-1, 0, 1) for t in range(date_size) if (o, t) != (0, 0)]

    barrier = pltpu.get_barrier_semaphore()
    pl.semaphore_signal(barrier, inc=1, device_id=other_core, device_id_type=MESH)
    for o, t in peers:
        if o >= 0:
            @pl.when(jnp.logical_and(jnp.logical_not(wraps[t]), has_down if o else True))
            def _(o=o, t=t):
                pl.semaphore_signal(barrier, inc=1, device_id=place_at(o, t), device_id_type=MESH)
    for load in loads[:3]:
        load.start()

    coarse = jnp.zeros((2, REACH - FINE, samples), near.dtype)
    near[1, :, 0 : REACH - FINE] = coarse
    near[1, :, REACH + lines + FINE :] = coarse

    @pl.when(jnp.logical_not(has_up))
    def _():
        near[0, :, 0 : REACH - FINE] = coarse
        margin[0] = jnp.zeros(margin.shape[1:], margin.dtype)
        far[:, :, 0:REACH] = jnp.zeros((date_size - 1, 2, REACH, samples), far.dtype)
        all_kernels[:, 0] = jnp.zeros((date_size,) + all_kernels.shape[2:], jnp.float32)

    @pl.when(jnp.logical_not(has_down))
    def _():
        near[0, :, REACH + lines + FINE :] = coarse
        margin[1] = jnp.zeros(margin.shape[1:], margin.dtype)
        far[:, :, REACH + lines :] = jnp.zeros((date_size - 1, 2, REACH, samples), far.dtype)
        all_kernels[:, 2] = jnp.zeros((date_size,) + all_kernels.shape[2:], jnp.float32)

    no_side = jnp.zeros((date_size, HALF, ifg.shape[2]), ifg.dtype)

    @pl.when(g == 0)
    def _():
        ifg[:, 0:HALF] = no_side

    @pl.when(g != 0)
    def _():
        ifg[:, HALF + samples :] = no_side

    taken = {
        1: (lines - REACH, REACH, 0), 0: (0, lines, REACH), -1: (0, REACH, REACH + lines),
    }

    def send(o, t, kind, target):
        slot = (date_size - t) % date_size
        spot = PLACE[o]
        first, size, land = taken[o]
        if kind == 0 and t == 0:
            src = image_hbm.at[:, 0, pl.ds(lines - FINE if o == 1 else 0, FINE), :]
            dst = margin.at[0 if o == 1 else 1]
        elif kind == 2:
            skip = 0 if o == 1 else FINE
            src = tile.at[:, pl.ds(first + skip, REACH - FINE), :]
            dst = near.at[0, :, pl.ds(land + skip, REACH - FINE), :]
        elif kind == 0:
            src = tile.at[:, pl.ds(first, size), :]
            dst = far.at[slot - 1, :, pl.ds(land, size), :]
        else:
            src, dst = kernels, all_kernels.at[slot, spot]
        return pltpu.make_async_remote_copy(
            src_ref=src, dst_ref=dst,
            send_sem=send_sem.at[t, spot, kind],
            recv_sem=recv_sem.at[slot, spot, kind],
            device_id=target, device_id_type=MESH,
        )

    def push(o, t, kind):
        send(o, t, kind, place_at(o, t)).start()

    pl.semaphore_wait(barrier, has_up.astype(jnp.int32) * (d + 1) + d + 1)
    for o, t in peers:
        if o <= 0:
            @pl.when(jnp.logical_and(wraps[t] if t else True, has_up if o else True))
            def _(o=o, t=t):
                pl.semaphore_signal(
                    ready.at[PLACE[-o], (date_size - t) % date_size], inc=1,
                    device_id=place_at(o, t), device_id_type=MESH)

    leads = jnp.logical_or(d == 0, g == 1)

    @pl.when(jnp.logical_and(has_up, leads))
    def _():
        push(-1, 0, 0)

    for load in loads[:2]:
        load.wait()
    shifts = jnp.broadcast_to(offsets[0:1, :].astype(jnp.float32), (TAPS, lines))
    held = jnp.concatenate([taps[:, 0], shifts], axis=1)
    kernels[...] = held
    all_kernels[0, 1] = held

    @pl.when(jnp.logical_and(has_up, leads))
    def _():
        push(-1, 0, 1)

    loads[2].wait()
    for c in range(2):
        tile[c] = image[c, 0].astype(jnp.bfloat16)
    for t in range(1, date_size):
        @pl.when(wraps[t])
        def _(t=t):
            @pl.when(has_up)
            def _():
                push(-1, t, 1)
                push(-1, t, 0)

            push(0, t, 1)
            push(0, t, 0)

    @pl.when(has_up)
    def _():
        push(-1, 0, 2)

    @pl.when(jnp.logical_and(has_up, jnp.logical_not(leads)))
    def _():
        push(-1, 0, 1)
        push(-1, 0, 0)

    for load in loads[3:]:
        load.start()
    for c in range(2):
        value = image[c, 0]
        high = value.astype(jnp.bfloat16)
        near[0, c, REACH : REACH + lines] = high
        near[1, c, REACH : REACH + lines] = (value - high.astype(jnp.float32)).astype(jnp.bfloat16)

    for t in range(1, date_size):
        @pl.when(jnp.logical_not(wraps[t]))
        def _(t=t):
            pl.semaphore_wait(ready.at[PLACE[0], t], 1)
            @pl.when(has_up)
            def _():
                push(-1, t, 1)
                push(-1, t, 0)

            push(0, t, 1)
            push(0, t, 0)

    @pl.when(has_down)
    def _():
        pl.semaphore_wait(ready.at[PLACE[1], 0], 1)
        for t in range(1, date_size):
            @pl.when(wraps[t])
            def _(t=t):
                push(1, t, 1)
                push(1, t, 0)

        push(1, 0, 1)
        push(1, 0, 0)
        push(1, 0, 2)
        for t in range(1, date_size):
            @pl.when(jnp.logical_not(wraps[t]))
            def _(t=t):
                pl.semaphore_wait(ready.at[PLACE[1], t], 1)
                push(1, t, 1)
                push(1, t, 0)

    def arrived(slot, kinds):
        t = (date_size - slot) % date_size
        for o in (-1, 0, 1):
            if (o, t) != (0, 0):
                def _(o=o):
                    for kind in kinds:
                        send(o, t, kind, place_at(-o, slot)).wait_recv()
                guarded(-o, _)

    def side(slot):
        return pltpu.make_async_remote_copy(
            src_ref=ifg.at[slot, pl.ds(pl.multiple_of(samples - (samples - HALF) * g, HALF), HALF)],
            dst_ref=ifg.at[slot, pl.ds(pl.multiple_of((samples + HALF) * g, HALF), HALF)],
            send_sem=side_sem.at[0, slot], recv_sem=side_sem.at[1, slot],
            device_id=other_core, device_id_type=MESH,
        )

    def side_arrived(slot):
        pltpu.make_async_remote_copy(
            src_ref=ifg.at[slot, pl.ds(pl.multiple_of(samples - (samples - HALF) * g, HALF), HALF)],
            dst_ref=ifg.at[slot, pl.ds(pl.multiple_of((samples + HALF) * (1 - g), HALF), HALF)],
            send_sem=side_sem.at[0, slot], recv_sem=side_sem.at[1, slot],
            device_id=other_core, device_id_type=MESH,
        ).wait_recv()

    span = lines + 2 * REACH
    wide_lines = 4 * HALF
    source = lax.broadcasted_iota(jnp.int32, (span, wide_lines), 0)
    place = lax.broadcasted_iota(jnp.int32, (span, wide_lines), 1)
    distance = (source - place - (RIM - (TAPS // 2 - 1))).astype(jnp.float32)

    def make_band(slot):
        above, own_rows, below = (all_kernels[slot, i] for i in range(3))
        weights = jnp.concatenate(
            [above[:, HALF:lines], own_rows[:, :lines], below[:, :HALF]], axis=1
        )
        shift = jnp.concatenate(
            [above[:, lines + HALF :], own_rows[:, lines:], below[:, lines : lines + HALF]], axis=1
        )
        gap = distance - shift[0:1]
        band = jnp.zeros((span, wide_lines), jnp.float32)
        for k in range(TAPS):
            band = jnp.where(gap == float(k), weights[k : k + 1], band)
        band_high = band.astype(jnp.bfloat16)
        band_low = (band - band_high.astype(jnp.float32)).astype(jnp.bfloat16)
        bands[slot] = jnp.concatenate([band_high, band_low], axis=1)

    def resample(slot, pieces, at, size):
        total = None
        for piece in pieces:
            columns = [piece[c, :, pl.ds(at, size)] for c in range(2)]
            product = lax.dot_general(
                jnp.concatenate(columns, axis=1), bands[slot], (((0,), (0,)), ((), ())),
                preferred_element_type=jnp.float32,
            )
            product = product[:, :wide_lines] + product[:, wide_lines:]
            total = product if total is None else total + product
        total = total.astype(jnp.bfloat16).astype(jnp.float32)
        return total[:size], total[size:]

    def store(slot, at, real_part, imag_part):
        rows = pl.ds(at, real_part.shape[0])
        ifg[slot, rows, :wide_lines] = real_part.astype(jnp.bfloat16)
        ifg[slot, rows, wide_lines:] = imag_part.astype(jnp.bfloat16)

    def take_own():
        arrived(0, (1, 0, 2))
        make_band(0)
        for i in range(2):
            for c in range(2):
                value = margin[i, c]
                high = value.astype(jnp.bfloat16)
                first = REACH - FINE if i == 0 else REACH + lines
                at = slice(first, first + FINE)
                near[0, c, at] = high
                near[1, c, at] = (value - high.astype(jnp.float32)).astype(jnp.bfloat16)
        real, imag = resample(0, [near.at[0], near.at[1]], 0, samples)
        own[0], own[1] = real, imag
        store(0, HALF, real * real + imag * imag, jnp.zeros_like(real))
        side(0).start()

    def take_other(slot):
        arrived(slot, (1,))
        make_band(slot)
        arrived(slot, (0,))
        size = samples // 2
        for i, half in enumerate((1 - g, g)):
            at = pl.multiple_of(half * size, size)
            real, imag = resample(slot, [far.at[slot - 1]], at, size)
            own_real, own_imag = own[0, pl.ds(at, size)], own[1, pl.ds(at, size)]
            store(
                slot, pl.multiple_of(at + HALF, HALF), own_real * real + own_imag * imag,
                own_imag * real - own_real * imag,
            )
            if i == 0:
                side(slot).start()

    take_own()
    for load in loads[3:]:
        load.wait()
    if date_size == 2:
        single = Filter(ifg.at[0], table, True, *kept[3:6], *scratch[3:], kept[6])
        single.lines(single.inside)
        single.samples(single.inner)
    for j in range(1, date_size):
        take_other(j)
    if date_size == 2:
        cross = Filter(ifg.at[1], table, False, *kept[:3], *scratch[:3])
        cross.lines(cross.inside)
        cross.samples(cross.inner)
        single.gain(single.inner)
        cross.gain(cross.inner)
        cross.samples_back_inner()
    for o, t in peers:
        def _(o=o, t=t):
            for kind in (1, 0) if t else (1, 0, 2):
                send(o, t, kind, place_at(o, t)).wait_send()
        guarded(o, _)
    for j in range(date_size):
        side_arrived(j)
    for slot in range(date_size):
        side(slot).wait_send()


def filter_kernel(date_size, ifg, table, by_date, *rest):
    alone = date_size == 2
    kept, rest = (rest[:7], rest[7:]) if alone else ([], rest)
    out, results, partner, sem, read_sem, *rest = rest
    kept, scratch = (kept, rest) if alone else (rest[:3], rest[3:])
    matches = out.shape[0]
    d = lax.axis_index("date")
    read = pltpu.make_async_copy(by_date, partner, read_sem)
    read.start()

    def deliver(m, c, spot):
        return pltpu.make_async_copy(
            results.at[spot, pl.ds(c * PATCH, PATCH)], out.at[m, c, 0], sem.at[m, c])

    if alone:
        results[0, PATCH:] = jnp.zeros((PATCH, results.shape[2]), results.dtype)
        cross = Filter(ifg.at[1], table, False, *kept[:3], *scratch[:3])
        single = Filter(ifg.at[0], table, True, *kept[3:6], *scratch[3:], kept[6])
        cross.lines(cross.outside)
        single.lines(single.outside)
        single.samples_back_inner()
        results[0, :PATCH], results[1] = finish_outer(single, cross)
        read.wait()
        for m in range(matches):
            spot = lax.rem(partner[d, m] - d + date_size, date_size)
            for c in range(2):
                deliver(m, c, spot).start()
    else:
        read.wait()
        for m in range(matches):
            spot = lax.rem(partner[d, m] - d + date_size, date_size)
            one = Filter(ifg.at[spot], table, False, *kept, *scratch)
            run_inner(one)
            results[m] = run_outer(one)[0]
            for c in range(2):
                deliver(m, c, m).start()
    for m in range(matches):
        for c in range(2):
            deliver(m, c, 0).wait()


def per_device(az_size, date_size, image_stack, tap_weights, offsets, matchings):
    lines, samples = image_stack.shape[2:]
    assert image_stack.shape[1] == 1 and lines == PATCH
    matches = matchings.shape[0]
    hbm = pl.BlockSpec(memory_space=pltpu.HBM)
    vmem = pl.BlockSpec(memory_space=pltpu.VMEM)
    constants = tables()
    alone = date_size == 2
    passed = [
        pltpu.VMEM((date_size, samples + 2 * HALF, 8 * HALF), jnp.bfloat16),
        pltpu.VMEM(constants.shape, jnp.bfloat16),
        pltpu.VMEM((date_size, matches), jnp.int32),
    ]
    if alone:
        passed += kept_of_filter(samples, LANES) + kept_of_filter(samples, HALF_LANES)
        passed.append(scratch_of_filter(samples, HALF_LANES)[-1])
    scratch = scratch_of_filter(samples, LANES)
    if alone:
        scratch += scratch_of_filter(samples, HALF_LANES)[:-1]
    else:
        scratch = kept_of_filter(samples, LANES) + scratch
    passed = pl.pallas_call(
        functools.partial(stack_kernel, az_size, date_size),
        out_shape=passed,
        in_specs=[hbm] * 5,
        out_specs=[vmem] * len(passed),
        scratch_shapes=(scratch if alone else []) + [
            pltpu.VMEM(image_stack.shape, jnp.float32),
            pltpu.VMEM(tap_weights.shape, jnp.float32),
            pltpu.VMEM(offsets.shape, jnp.int32),
            pltpu.VMEM((2, lines, samples), jnp.bfloat16),
            pltpu.VMEM((TAPS, 2 * lines), jnp.float32),
            pltpu.VMEM((2, 2, lines + 2 * REACH, samples), jnp.bfloat16),
            pltpu.VMEM((date_size - 1, 2, lines + 2 * REACH, samples), jnp.bfloat16),
            pltpu.VMEM((2, 2, FINE, samples), jnp.float32),
            pltpu.VMEM((date_size, 3, TAPS, 2 * lines), jnp.float32),
            pltpu.VMEM((date_size, lines + 2 * REACH, 8 * HALF), jnp.bfloat16),
            pltpu.VMEM((2, samples, 4 * HALF), jnp.float32),
            pltpu.SemaphoreType.DMA((5,)),
            pltpu.SemaphoreType.DMA((date_size, 3, 3)),
            pltpu.SemaphoreType.DMA((date_size, 3, 3)),
            pltpu.SemaphoreType.DMA((2, date_size)),
            pltpu.SemaphoreType.REGULAR((3, date_size)),
        ],
        compiler_params=pltpu.CompilerParams(collective_id=0, has_side_effects=True),
    )(image_stack, tap_weights, offsets, jnp.asarray(constants), matchings.T)
    return pl.pallas_call(
        functools.partial(filter_kernel, date_size),
        out_shape=jax.ShapeDtypeStruct((matches, 2, 1, lines, samples), jnp.float32),
        in_specs=[vmem] * len(passed),
        out_specs=hbm,
        scratch_shapes=[
            pltpu.VMEM((2 if alone else matches, 2 * lines, samples), jnp.float32),
            pltpu.SMEM((date_size, matches), jnp.int32),
            pltpu.SemaphoreType.DMA((matches, 2)),
            pltpu.SemaphoreType.DMA,
        ] + scratch,
        compiler_params=pltpu.CompilerParams(vmem_limit_bytes=24 << 20),
    )(*passed)


def solution(mesh):
    placed = (
        P(None, ("parts", "date"), "az", "rg"),
        P(None, ("parts", "date"), "az"),
        P(("parts", "date"), "az"),
        P(),
    )
    assert mesh.shape["rg"] == 2
    return jax.shard_map(
        functools.partial(per_device, mesh.shape["az"], mesh.shape["date"]),
        mesh=mesh,
        in_specs=placed,
        out_specs=P(None, None, ("parts", "date"), "az", "rg"),
        check_vma=False,
    )
```
